256 devices in a mesh: leaf: 256 (over y, z, x, core).
Axes of the slice: x: 4, y: 4, z: 8, core: 2. Of those that a mesh axis runs over, the one named last changes fastest.
Arguments:
- points: float32 [16, 524288], P(None, 'leaf'), may hold values from -6 to 6
- order: int32 [524288], P('leaf'), may hold values from 0 to 524287, as said below
- bases: float32 [2048, 256, 64], P('leaf'), may hold values from -0.375 to 0.375
- lift: float32 [2048, 64, 64], P('leaf'), may hold values from -0.25 to 0.25
- near_ids: int32 [2048, 3], P('leaf'), may hold values from 0 to 2047, as said below
- near_blocks: float32 [2048, 3, 256, 256], P('leaf'), may hold values from -0.21875 to 0.21875
- far_ids: int32 [2048, 8], P('leaf'), may hold values from 0 to 2047, as said below
- far_count: int32 [2048], P('leaf'), may hold values from 1 to 8
- far_blocks: float32 [2048, 8, 64, 64], P('leaf'), may hold values from -0.25 to 0.25
- transfer: float32 [4, 2, 64, 64], replicated, may hold values from -0.5 to 0.5
- couple: float32 [4, 4, 64, 64], replicated, may hold values from -0.375 to 0.375
- links: int32 [256, 4, 4], P('leaf'), may hold values from 0 to 1, as said below
- top_couple: float32 [64, 64], replicated, may hold values from -0.75 to 0.75
Outputs:
- product: float32 [16, 524288], P(None, 'leaf')
The draws below stay inside these ranges and needn't reach their ends.
Inputs may be any that keep to these rules, and one draw needn't show every extreme that they name: `order`: each subtree's 2048 entries are a permutation of that subtree's positions. `near_ids`: the first entry of a leaf is the leaf itself; the others lie at most one leaf away. `far_ids`: a coupled leaf lies in a subtree at most 4 subtrees away from the leaf's own; slots at or beyond far_count are padding. links[d, l, k] is the same for all d in one aligned block of 2^l subtrees.
All inputs are finite; a program needn't handle non-finite values.
Results may differ from the reference program's by a relative error of at most 0.0001.
Values sent between devices are 32-bit elements; how exact they have to be, the bound alone decides.
A program may use at most 64 MiB of HBM per device.

```python
import jax
import jax.numpy as jnp
from jax import lax

LEAF = 256
RANK = 64
RHS = 16
LEAF_DEV = 8
NEAR = 3
CPL = 8
REACH = 4
DEPTH = 4
PTS_DEV = 2048
LEAVES = 2048
POINTS = 524288
N_LEAF = 256


def draw_order(key, part):
    subkeys = jax.random.split(key, N_LEAF)
    shuffles = jax.vmap(lambda k: jax.random.permutation(k, PTS_DEV))(subkeys)
    offsets_dev = jnp.arange(N_LEAF, dtype=jnp.int32)[:, None] * PTS_DEV
    return (shuffles.astype(jnp.int32) + offsets_dev).reshape(-1)


def draw_near_ids(key, part):
    own_leaf = jnp.arange(LEAVES, dtype=jnp.int32)
    jumps = jax.random.randint(key, (LEAVES, NEAR - 1), -1, 2, dtype=jnp.int32)
    others = jnp.clip(own_leaf[:, None] + jumps, 0, LEAVES - 1)
    return jnp.concatenate([own_leaf[:, None], others], axis=1)


def draw_far_ids(key, part):
    own_device = jnp.arange(LEAVES, dtype=jnp.int32) // LEAF_DEV
    first_key, second_key = jax.random.split(jax.random.fold_in(key, 11))
    device_moves = jax.random.randint(first_key, (LEAVES, CPL), -REACH, REACH + 1, dtype=jnp.int32)
    target = jnp.clip(own_device[:, None] + device_moves, 0, N_LEAF - 1)
    within = jax.random.randint(second_key, (LEAVES, CPL), 0, LEAF_DEV, dtype=jnp.int32)
    partner = target * LEAF_DEV + within
    return partner.at[0, 0].set(REACH * LEAF_DEV)


def draw_far_count(key, part):
    counted = jax.random.randint(jax.random.fold_in(key, 23), (LEAVES,), 1, CPL + 1, dtype=jnp.int32)
    return counted.at[0].set(CPL).at[LEAVES - 1].set(1)


def draw_links(key, part):
    raw_bits = jax.random.randint(jax.random.fold_in(key, 37), (N_LEAF, DEPTH, 4), 0, 2, dtype=jnp.int32)
    devices = jnp.arange(N_LEAF, dtype=jnp.int32)[:, None]
    shifts = jnp.arange(DEPTH, dtype=jnp.int32)[None, :]
    block_start = jnp.left_shift(jnp.right_shift(devices, shifts), shifts)
    return raw_bits[block_start, shifts, :]


def block_levels(key, shape, pieces, low, high):
    loudness, own = 1.0, jax.random.fold_in(key, 6)
    for axis_at, blocks in pieces:
        heights = jnp.exp(jax.random.uniform(jax.random.fold_in(own, axis_at), (blocks,), jnp.float32, low / len(pieces), high / len(pieces)))
        loudness = loudness * jnp.repeat(heights, shape[axis_at] // blocks).reshape([-1 if axis == axis_at else 1 for axis in range(len(shape))])
    return loudness


def gaussian(stream_key, shape, scale, reach, shards=(), kind=jnp.bfloat16):
    factor_of = block_levels(stream_key, shape, shards, -0.22, 0.18) if shards else 1.0
    result = jax.random.normal(stream_key, shape, jnp.float32) * scale * factor_of
    return jnp.minimum(jnp.maximum(result, -reach), reach).astype(kind)


def setup_inputs(seed: int = 0) -> dict:
    arg_keys = jax.random.split(jax.random.key(seed), 14)
    return {
        "points": gaussian(arg_keys[0], (RHS, POINTS), 1.0, 6.0, ((1, 256),), jnp.float32),
        "order": draw_order(jax.random.fold_in(arg_keys[13], 71), 0),
        "bases": gaussian(arg_keys[2], (LEAVES, LEAF, RANK), LEAF ** -0.5, 0.375, ((0, 256),), jnp.float32),
        "lift": gaussian(arg_keys[3], (LEAVES, RANK, RANK), (RANK * LEAF_DEV) ** -0.5, 0.25, ((0, 256),), jnp.float32),
        "near_ids": draw_near_ids(jax.random.fold_in(arg_keys[13], 71), 0),
        "near_blocks": gaussian(arg_keys[5], (LEAVES, NEAR, LEAF, LEAF), (NEAR * LEAF) ** -0.5, 0.21875, ((0, 256),), jnp.float32),
        "far_ids": draw_far_ids(jax.random.fold_in(arg_keys[13], 71), 0),
        "far_count": draw_far_count(jax.random.fold_in(arg_keys[13], 71), 0),
        "far_blocks": gaussian(arg_keys[8], (LEAVES, CPL, RANK, RANK), (RANK * CPL) ** -0.5, 0.25, ((0, 256),), jnp.float32),
        "transfer": gaussian(arg_keys[9], (DEPTH, 2, RANK, RANK), (2 * RANK) ** -0.5, 0.5, (), jnp.float32),
        "couple": gaussian(arg_keys[10], (DEPTH, 4, RANK, RANK), (4 * RANK) ** -0.5, 0.375, (), jnp.float32),
        "links": draw_links(jax.random.fold_in(arg_keys[13], 71), 0),
        "top_couple": gaussian(arg_keys[12], (RANK, RANK), RANK ** -0.5, 0.75, (), jnp.float32),
    }


HIGHEST_PRECISION = lax.Precision.HIGHEST
OFFSETS = (-3, -2, 2, 3)


def full_tree(node_zero, link_table, transfer, couple, top_couple):
    levels = [node_zero]
    for level in range(DEPTH):
        current = levels[-1]
        paired = current.reshape(current.shape[0] // 2, 2, current.shape[1], current.shape[2])
        parent = jnp.einsum('rq,nrs->nqs', transfer[level, 0], paired[:, 0], precision=HIGHEST_PRECISION)
        parent = parent + jnp.einsum('rq,nrs->nqs', transfer[level, 1], paired[:, 1], precision=HIGHEST_PRECISION)
        levels.append(parent)
    couplings = []
    for level in range(DEPTH):
        current = levels[level]
        node_count = current.shape[0]
        chosen_links = link_table[::(1 << level), level, :].astype(jnp.float32)
        padded = jnp.pad(current, ((3, 3), (0, 0), (0, 0)))
        summed = jnp.zeros_like(current)
        for column, offset in enumerate(OFFSETS):
            partner = padded[3 + offset:3 + offset + node_count]
            term = jnp.einsum('qr,nrs->nqs', couple[level, column], partner, precision=HIGHEST_PRECISION)
            summed = summed + chosen_links[:, column][:, None, None] * term
        couplings.append(summed)
    top_nodes = levels[DEPTH]
    top_count = top_nodes.shape[0]
    spots = jnp.arange(top_count, dtype=jnp.int32)
    distance = jnp.abs(spots[:, None] - spots[None, :])
    weight = jnp.where(distance >= 2, 1.0 / jnp.maximum(distance, 1).astype(jnp.float32), 0.0).astype(jnp.float32)
    blended = jnp.einsum('nm,mrs->nrs', weight, top_nodes, precision=HIGHEST_PRECISION)
    downward = jnp.einsum('qr,nrs->nqs', top_couple, blended, precision=HIGHEST_PRECISION)
    for level in reversed(range(DEPTH)):
        even_part = jnp.einsum('rq,nqs->nrs', transfer[level, 0], downward, precision=HIGHEST_PRECISION)
        odd_part = jnp.einsum('rq,nqs->nrs', transfer[level, 1], downward, precision=HIGHEST_PRECISION)
        spread = jnp.stack([even_part, odd_part], axis=1).reshape(-1, downward.shape[1], downward.shape[2])
        downward = couplings[level] + spread
    return downward


def reference(points, order, bases, lift, near_ids, near_blocks, far_ids, far_count, far_blocks, transfer, couple, links, top_couple):
    vectors = points.shape[0]
    leaves = bases.shape[0]
    tree_x = jnp.take(points, order, axis=1)
    blocks = tree_x.reshape(vectors, leaves, LEAF)
    leaf_coef = jnp.einsum('lpr,slp->lrs', bases, blocks, precision=HIGHEST_PRECISION)
    lifted = jnp.einsum('lrq,lrs->lqs', lift, leaf_coef, precision=HIGHEST_PRECISION)
    node_zero = lifted.reshape(N_LEAF, LEAF_DEV, RANK, vectors).sum(axis=1)
    down_zero = full_tree(node_zero, links, transfer, couple, top_couple)
    down_leaf = jnp.repeat(down_zero, LEAF_DEV, axis=0)
    picked = jnp.take(leaf_coef, far_ids, axis=0)
    active = (jnp.arange(CPL, dtype=jnp.int32)[None, :] < far_count[:, None]).astype(jnp.float32)
    picked = picked * active[:, :, None, None]
    far_part = jnp.einsum('lkrq,lkqs->lrs', far_blocks, picked, precision=HIGHEST_PRECISION)
    leaf_out = jnp.einsum('lrq,lqs->lrs', lift, down_leaf, precision=HIGHEST_PRECISION) + far_part
    gathered = jnp.take(blocks, near_ids, axis=1)
    near_part = jnp.einsum('lkpq,slkq->slp', near_blocks, gathered, precision=HIGHEST_PRECISION)
    tree_y = near_part + jnp.einsum('lpr,lrs->slp', bases, leaf_out, precision=HIGHEST_PRECISION)
    tree_y = tree_y.reshape(vectors, -1)
    return jnp.zeros_like(points).at[:, order].set(tree_y)
```

```python
import jax
import jax.numpy as jnp
from jax import lax
from jax.sharding import PartitionSpec as P

REACH = 4
DEPTH = 4


HIGHEST_PRECISION = lax.Precision.HIGHEST
OFFSETS = (-3, -2, 2, 3)


def extended_2(block, sides, width):
    for axis, dim in sides:
        count = lax.axis_size(axis)
        forward = [(i, i + 1) for i in range(count - 1)]
        backward = [(target, source) for source, target in forward]
        low = lax.ppermute(
            lax.slice_in_dim(block, block.shape[dim] - width, None, axis=dim), axis, forward
        )
        high = lax.ppermute(lax.slice_in_dim(block, 0, width, axis=dim), axis, backward)
        block = jnp.concatenate([low, block, high], axis=dim)
    return block


def from_behind(x, axis, by):
    count = lax.axis_size(axis)
    pairs = [(i, i + by) for i in range(count) if 0 <= i + by < count]
    return lax.ppermute(x, axis, pairs)


def mat_t(m, x):
    return jnp.einsum("rq,rs->qs", m, x, precision=HIGHEST_PRECISION)


def mat(m, x):
    return jnp.einsum("qr,rs->qs", m, x, precision=HIGHEST_PRECISION)


def tree_down(node_zero, my_links, transfer, couple, top_couple, position, count):
    levels = [node_zero]
    node = node_zero
    for level in range(DEPTH):
        stride = 1 << level
        partner = lax.ppermute(node, "leaf", [(i, i ^ stride) for i in range(count)])
        bit = (position >> level) & 1
        own_t = transfer[level][bit]
        other_t = transfer[level][1 - bit]
        node = mat_t(own_t, node) + mat_t(other_t, partner)
        levels.append(node)
    couplings = []
    for level in range(DEPTH):
        stride = 1 << level
        summed = jnp.zeros_like(node_zero)
        for column, offset in enumerate(OFFSETS):
            shift = offset * stride
            pairs = [(i + shift, i) for i in range(count) if 0 <= i + shift < count]
            partner = lax.ppermute(levels[level], "leaf", pairs)
            term = mat(couple[level, column], partner)
            summed = summed + my_links[level, column].astype(jnp.float32) * term
        couplings.append(summed)
    gathered = levels[DEPTH][None]
    top_count = count >> DEPTH
    step = 0
    while (1 << step) < top_count:
        stride = 1 << (DEPTH + step)
        other = lax.ppermute(gathered, "leaf", [(i, i ^ stride) for i in range(count)])
        upper = ((position >> (DEPTH + step)) & 1) == 1
        gathered = jnp.where(
            upper,
            jnp.concatenate([other, gathered], axis=0),
            jnp.concatenate([gathered, other], axis=0),
        )
        step += 1
    top_index = position >> DEPTH
    spots = jnp.arange(top_count, dtype=jnp.int32)
    distance = jnp.abs(spots - top_index)
    weight = jnp.where(distance >= 2, 1.0 / jnp.maximum(distance, 1).astype(jnp.float32), 0.0)
    blended = jnp.einsum("m,mrs->rs", weight, gathered, precision=HIGHEST_PRECISION)
    downward = mat(top_couple, blended)
    for level in reversed(range(DEPTH)):
        bit = (position >> level) & 1
        downward = couplings[level] + mat(transfer[level][bit], downward)
    return downward


def local(
    points,
    order,
    bases,
    lift,
    near_ids,
    near_blocks,
    far_ids,
    far_count,
    far_blocks,
    transfer,
    couple,
    links,
    top_couple,
):
    position = lax.axis_index("leaf")
    count = lax.axis_size("leaf")
    vectors, points_dev = points.shape
    leaf_dev, leaf_size, rank_size = bases.shape
    local_order = order - position * points_dev
    tree_x = jnp.take(points, local_order, axis=1)
    blocks = tree_x.reshape(vectors, leaf_dev, leaf_size)
    leaf_coef = jnp.einsum("lpr,slp->lrs", bases, blocks, precision=HIGHEST_PRECISION)
    node_zero = jnp.einsum("lrq,lrs->qs", lift, leaf_coef, precision=HIGHEST_PRECISION)
    down_zero = tree_down(node_zero, links[0], transfer, couple, top_couple, position, count)
    extended = extended_2(tree_x, (("leaf", 1),), leaf_size)
    extended = extended.reshape(vectors, leaf_dev + 2, leaf_size)
    near_local = near_ids - position * leaf_dev + 1
    gathered = jnp.take(extended, near_local, axis=1)
    near_part = jnp.einsum("lkpq,slkq->slp", near_blocks, gathered, precision=HIGHEST_PRECISION)
    pieces = []
    for offset in range(-REACH, REACH + 1):
        if offset == 0:
            pieces.append(leaf_coef)
        else:
            pieces.append(from_behind(leaf_coef, "leaf", -offset))
    window = jnp.stack(pieces).reshape((2 * REACH + 1) * leaf_dev, rank_size, vectors)
    window_slot = (far_ids // leaf_dev - position + REACH) * leaf_dev + far_ids % leaf_dev
    picked = jnp.take(window, window_slot, axis=0)
    active = (jnp.arange(far_ids.shape[1], dtype=jnp.int32)[None, :] < far_count[:, None]).astype(
        jnp.float32
    )
    picked = picked * active[:, :, None, None]
    far_part = jnp.einsum("lkrq,lkqs->lrs", far_blocks, picked, precision=HIGHEST_PRECISION)
    leaf_out = jnp.einsum("lrq,qs->lrs", lift, down_zero, precision=HIGHEST_PRECISION) + far_part
    tree_y = near_part + jnp.einsum("lpr,lrs->slp", bases, leaf_out, precision=HIGHEST_PRECISION)
    tree_y = tree_y.reshape(vectors, points_dev)
    return jnp.zeros((vectors, points_dev), jnp.float32).at[:, local_order].set(tree_y)


def solution(mesh):
    in_specs = (
        P(None, "leaf"),
        P("leaf"),
        P("leaf", None, None),
        P("leaf", None, None),
        P("leaf", None),
        P("leaf", None, None, None),
        P("leaf", None),
        P("leaf"),
        P("leaf", None, None, None),
        P(),
        P(),
        P("leaf", None, None),
        P(),
    )
    out_specs = P(None, "leaf")
    return jax.shard_map(local, mesh=mesh, in_specs=in_specs, out_specs=out_specs, check_vma=False)
```

```python
import functools

import jax
import jax.numpy as jnp
from jax import lax
from jax.experimental import pallas as pl
from jax.experimental.pallas import tpu as pltpu
from jax.sharding import PartitionSpec as P

REACH = 4
DEPTH = 4
NODE_REACH = 4 * (1 << (DEPTH - 1)) - 1

HIGHEST_PRECISION = lax.Precision.HIGHEST
OFFSETS = (-3, -2, 2, 3)
MESH_ID = pl.DeviceIdType.MESH


def halo_kernel(count, node_ref, coef_ref, lo_ref, hi_ref,
                node_out, coef_out, edge_out,
                node_buf, coef_buf, edge_buf, send_sem, recv_sem):
    me = lax.axis_index("leaf")
    barrier = pltpu.get_barrier_semaphore()
    for k in range(1, NODE_REACH + 1):
        for dest in ((me + k) % count, (me + count - k) % count):
            pl.semaphore_signal(barrier, inc=1, device_id=(dest,), device_id_type=MESH_ID)
    pl.semaphore_wait(barrier, 2 * NODE_REACH)

    copies = []

    def push(src, dst, dest):
        index = len(copies)
        copy = pltpu.make_async_remote_copy(
            src_ref=src, dst_ref=dst, send_sem=send_sem.at[index],
            recv_sem=recv_sem.at[index], device_id=(dest,), device_id_type=MESH_ID)
        copy.start()
        copies.append(copy)

    push(hi_ref, edge_buf.at[0], (me + 1) % count)
    push(lo_ref, edge_buf.at[1], (me + count - 1) % count)
    for k in range(1, REACH + 1):
        push(coef_ref, coef_buf.at[REACH - k], (me + k) % count)
        push(coef_ref, coef_buf.at[REACH + k], (me + count - k) % count)
    for k in range(1, NODE_REACH + 1):
        push(node_ref, node_buf.at[NODE_REACH - k], (me + k) % count)
        push(node_ref, node_buf.at[NODE_REACH + k], (me + count - k) % count)
    node_buf[NODE_REACH] = node_ref[...]
    coef_buf[REACH] = coef_ref[...]
    for copy in copies:
        copy.wait()
    node_out[...] = node_buf[...]
    coef_out[...] = coef_buf[...]
    edge_out[...] = edge_buf[...]


def halo_exchange(node_flat, coef_flat, lo, hi, count):
    n_copies = 2 + 2 * REACH + 2 * NODE_REACH
    vmem = pl.BlockSpec(memory_space=pltpu.VMEM)
    return pl.pallas_call(
        functools.partial(halo_kernel, count),
        out_shape=(
            jax.ShapeDtypeStruct((2 * NODE_REACH + 1,) + node_flat.shape, jnp.float32),
            jax.ShapeDtypeStruct((2 * REACH + 1,) + coef_flat.shape, jnp.float32),
            jax.ShapeDtypeStruct((2,) + lo.shape, jnp.float32),
        ),
        in_specs=[vmem] * 4,
        out_specs=(vmem, vmem, vmem),
        scratch_shapes=[
            pltpu.VMEM((2 * NODE_REACH + 1,) + node_flat.shape, jnp.float32),
            pltpu.VMEM((2 * REACH + 1,) + coef_flat.shape, jnp.float32),
            pltpu.VMEM((2,) + lo.shape, jnp.float32),
            pltpu.SemaphoreType.DMA((n_copies,)),
            pltpu.SemaphoreType.DMA((n_copies,)),
        ],
        compiler_params=pltpu.CompilerParams(collective_id=0, has_side_effects=True),
    )(node_flat, coef_flat, lo, hi)


def top_kernel(count, top_count, node_ref, top_out, top_buf, send_sem, recv_sem):
    me = lax.axis_index("leaf")
    stride = count // top_count
    barrier = pltpu.get_barrier_semaphore()
    for k in range(1, top_count):
        pl.semaphore_signal(barrier, inc=1, device_id=((me + k * stride) % count,),
                            device_id_type=MESH_ID)
    pl.semaphore_wait(barrier, top_count - 1)
    copies = []
    for k in range(1, top_count):
        copy = pltpu.make_async_remote_copy(
            src_ref=node_ref, dst_ref=top_buf.at[k], send_sem=send_sem.at[k - 1],
            recv_sem=recv_sem.at[k - 1], device_id=((me + k * stride) % count,),
            device_id_type=MESH_ID)
        copy.start()
        copies.append(copy)
    top_buf[0] = node_ref[...]
    for copy in copies:
        copy.wait()
    top_out[...] = top_buf[...]


def top_exchange(node_flat, count, top_count):
    vmem = pl.BlockSpec(memory_space=pltpu.VMEM)
    return pl.pallas_call(
        functools.partial(top_kernel, count, top_count),
        out_shape=jax.ShapeDtypeStruct((top_count,) + node_flat.shape, jnp.float32),
        in_specs=[vmem],
        out_specs=vmem,
        scratch_shapes=[
            pltpu.VMEM((top_count,) + node_flat.shape, jnp.float32),
            pltpu.SemaphoreType.DMA((top_count - 1,)),
            pltpu.SemaphoreType.DMA((top_count - 1,)),
        ],
        compiler_params=pltpu.CompilerParams(collective_id=1, has_side_effects=True),
    )(node_flat)


def mat(m, x):
    return jnp.einsum("qr,rs->qs", m, x, precision=HIGHEST_PRECISION)


def up_pairs(transfer_level, nodes):
    paired = nodes.reshape(nodes.shape[0] // 2, 2, nodes.shape[1], nodes.shape[2])
    parent = jnp.einsum("rq,nrs->nqs", transfer_level[0], paired[:, 0], precision=HIGHEST_PRECISION)
    return parent + jnp.einsum("rq,nrs->nqs", transfer_level[1], paired[:, 1], precision=HIGHEST_PRECISION)


def local(
    points,
    order,
    bases,
    lift,
    near_ids,
    near_blocks,
    far_ids,
    far_count,
    far_blocks,
    transfer,
    couple,
    links,
    top_couple,
):
    position = lax.axis_index("leaf")
    count = lax.axis_size("leaf")
    vectors, points_dev = points.shape
    leaf_dev, leaf_size, rank_size = bases.shape
    local_order = order - position * points_dev
    tree_x = jnp.take(points, local_order, axis=1)
    blocks = tree_x.reshape(vectors, leaf_dev, leaf_size)
    leaf_coef = jnp.einsum("lpr,slp->lrs", bases, blocks, precision=HIGHEST_PRECISION)
    node_zero = jnp.einsum("lrq,lrs->qs", lift, leaf_coef, precision=HIGHEST_PRECISION)

    node_win, coef_win, edges = halo_exchange(
        node_zero.reshape(-1, 128),
        leaf_coef.reshape(-1, 128),
        tree_x[:, :leaf_size],
        tree_x[:, points_dev - leaf_size:],
        count,
    )
    node_win = node_win.reshape(2 * NODE_REACH + 1, rank_size, vectors)
    source = position - NODE_REACH + jnp.arange(2 * NODE_REACH + 1, dtype=jnp.int32)
    valid = (source >= 0) & (source < count)
    node_win = jnp.where(valid[:, None, None], node_win, 0.0)
    span = 1 << (DEPTH - 1)
    low = position % span
    aligned = lax.dynamic_slice_in_dim(node_win, (NODE_REACH - 3 * span) - low, 7 * span, axis=0)
    levels = [aligned]
    for level in range(DEPTH - 1):
        levels.append(up_pairs(transfer[level], levels[-1]))
    my_links = links[0]
    couplings = []
    for level in range(DEPTH):
        centre = (low >> level) + (3 * span >> level)
        partners = jnp.stack([
            lax.dynamic_index_in_dim(levels[level], centre + offset, 0, keepdims=False)
            for offset in OFFSETS
        ])
        partners = partners * my_links[level][:, None, None].astype(jnp.float32)
        couplings.append(jnp.einsum("kqr,krs->qs", couple[level], partners, precision=HIGHEST_PRECISION))
    top_level = levels[DEPTH - 1]
    first = 3 - ((position >> (DEPTH - 1)) & 1)
    even_child = lax.dynamic_index_in_dim(top_level, first, 0, keepdims=False)
    odd_child = lax.dynamic_index_in_dim(top_level, first + 1, 0, keepdims=False)
    node_top = (
        jnp.einsum("rq,rs->qs", transfer[DEPTH - 1, 0], even_child, precision=HIGHEST_PRECISION)
        + jnp.einsum("rq,rs->qs", transfer[DEPTH - 1, 1], odd_child, precision=HIGHEST_PRECISION)
    )
    top_count = count >> DEPTH
    gathered = top_exchange(node_top.reshape(-1, 128), count, top_count)
    gathered = gathered.reshape(top_count, rank_size, vectors)
    top_index = position >> DEPTH
    ks = jnp.arange(top_count, dtype=jnp.int32)
    partner_index = (top_index - ks + top_count) % top_count
    distance = jnp.abs(partner_index - top_index)
    weight = jnp.where(distance >= 2, 1.0 / jnp.maximum(distance, 1).astype(jnp.float32), 0.0)
    blended = jnp.einsum("m,mrs->rs", weight, gathered, precision=HIGHEST_PRECISION)
    down_zero = mat(top_couple, blended)
    for level in reversed(range(DEPTH)):
        bit = (position >> level) & 1
        down_zero = couplings[level] + mat(transfer[level][bit], down_zero)

    extended = jnp.concatenate([edges[0], tree_x, edges[1]], axis=1)
    extended = extended.reshape(vectors, leaf_dev + 2, leaf_size)
    near_local = near_ids - position * leaf_dev + 1
    gathered_near = jnp.take(extended, near_local, axis=1)
    near_part = jnp.einsum("lkpq,slkq->slp", near_blocks, gathered_near, precision=HIGHEST_PRECISION)
    window = coef_win.reshape((2 * REACH + 1) * leaf_dev, rank_size, vectors)
    window_slot = (far_ids // leaf_dev - position + REACH) * leaf_dev + far_ids % leaf_dev
    picked = jnp.take(window, window_slot, axis=0)
    active = (jnp.arange(far_ids.shape[1], dtype=jnp.int32)[None, :] < far_count[:, None]).astype(
        jnp.float32
    )
    picked = picked * active[:, :, None, None]
    far_part = jnp.einsum("lkrq,lkqs->lrs", far_blocks, picked, precision=HIGHEST_PRECISION)
    leaf_out = jnp.einsum("lrq,qs->lrs", lift, down_zero, precision=HIGHEST_PRECISION) + far_part
    tree_y = near_part + jnp.einsum("lpr,lrs->slp", bases, leaf_out, precision=HIGHEST_PRECISION)
    tree_y = tree_y.reshape(vectors, points_dev)
    return jnp.zeros((vectors, points_dev), jnp.float32).at[:, local_order].set(tree_y)


def solution(mesh):
    in_specs = (
        P(None, "leaf"),
        P("leaf"),
        P("leaf", None, None),
        P("leaf", None, None),
        P("leaf", None),
        P("leaf", None, None, None),
        P("leaf", None),
        P("leaf"),
        P("leaf", None, None, None),
        P(),
        P(),
        P("leaf", None, None),
        P(),
    )
    out_specs = P(None, "leaf")
    return jax.shard_map(local, mesh=mesh, in_specs=in_specs, out_specs=out_specs, check_vma=False)
```

```python
import functools

import jax
import jax.numpy as jnp
from jax import lax
from jax.experimental import pallas as pl
from jax.experimental.pallas import tpu as pltpu
from jax.sharding import PartitionSpec as P

REACH = 4
DEPTH = 4
NODE_REACH = 4 * (1 << (DEPTH - 1)) - 1

HIGHEST_PRECISION = lax.Precision.HIGHEST
OFFSETS = (-3, -2, 2, 3)
MESH_ID = pl.DeviceIdType.MESH


def nt_dot(x, y):
    return lax.dot_general(x, y, (((1,), (1,)), ((), ())), precision=HIGHEST_PRECISION,
                           preferred_element_type=jnp.float32)


def nn_dot(x, y):
    return jnp.dot(x, y, precision=HIGHEST_PRECISION, preferred_element_type=jnp.float32)


def up_level(nodes, t_even, t_odd):
    half, vectors, rank = nodes.shape[0] // 2, nodes.shape[1], nodes.shape[2]
    paired = nodes.reshape(half, 2 * vectors, rank)
    even = paired[:, :vectors].reshape(half * vectors, rank)
    odd = paired[:, vectors:].reshape(half * vectors, rank)
    return (nn_dot(even, t_even) + nn_dot(odd, t_odd)).reshape(half, vectors, rank)


def tree_kernel(count, top_count,
                node_ref, coef_ref, lo_ref, hi_ref, transfer_ref, couple_ref, top_couple_ref,
                links_ref, weight_ref,
                down_out, coef_out, edge_out,
                node_buf, coef_buf, edge_buf, top_buf, lvl1, lvl2, lvl3,
                send_sem, recv_sem, top_send, top_recv):
    me = lax.axis_index("leaf")
    stride = count // top_count
    barrier = pltpu.get_barrier_semaphore()
    targets = []
    for k in range(1, NODE_REACH + 1):
        targets += [(me + k) % count, (me + count - k) % count]
    for k in range(2, top_count - 1):
        if k * stride > NODE_REACH and count - k * stride > NODE_REACH:
            targets.append((me + k * stride) % count)
    for dest in targets:
        pl.semaphore_signal(barrier, inc=1, device_id=(dest,), device_id_type=MESH_ID)
    pl.semaphore_wait(barrier, len(targets))

    copies = []

    def push(src, dst, dest):
        index = len(copies)
        copy = pltpu.make_async_remote_copy(
            src_ref=src, dst_ref=dst, send_sem=send_sem.at[index],
            recv_sem=recv_sem.at[index], device_id=(dest,), device_id_type=MESH_ID)
        copy.start()
        copies.append(copy)

    push(hi_ref, edge_buf.at[0], (me + 1) % count)
    push(lo_ref, edge_buf.at[1], (me + count - 1) % count)
    for k in range(1, REACH + 1):
        push(coef_ref, coef_buf.at[REACH - k], (me + k) % count)
        push(coef_ref, coef_buf.at[REACH + k], (me + count - k) % count)
    for k in range(1, NODE_REACH + 1):
        push(node_ref, node_buf.at[NODE_REACH - k], (me + k) % count)
        push(node_ref, node_buf.at[NODE_REACH + k], (me + count - k) % count)
    node_buf[NODE_REACH] = node_ref[...]
    coef_buf[REACH] = coef_ref[...]
    for copy in copies:
        copy.wait()
    coef_out[...] = coef_buf[...]
    edge_out[...] = edge_buf[...]

    span = 1 << (DEPTH - 1)
    low = me % span
    width = 7 * span
    start = NODE_REACH - 3 * span - low
    aligned = node_buf[pl.ds(start, width)]
    source = me - NODE_REACH + start + lax.broadcasted_iota(jnp.int32, aligned.shape, 0)
    aligned = jnp.where((source >= 0) & (source < count), aligned, 0.0)
    lvl1[...] = up_level(aligned, transfer_ref[0, 0], transfer_ref[0, 1])
    lvl2[...] = up_level(lvl1[...], transfer_ref[1, 0], transfer_ref[1, 1])
    lvl3[...] = up_level(lvl2[...], transfer_ref[2, 0], transfer_ref[2, 1])

    couplings = []
    for level in range(DEPTH):
        centre = (low >> level) + ((3 * span) >> level)
        total = None
        for column, offset in enumerate(OFFSETS):
            if level == 0:
                partner = node_buf[NODE_REACH + offset]
                inside = (me + offset >= 0) & (me + offset < count)
                partner = jnp.where(inside, partner, 0.0)
            else:
                partner = (lvl1, lvl2, lvl3)[level - 1][centre + offset]
            scale = links_ref[level, column].astype(jnp.float32)
            term = nt_dot(partner, couple_ref[level, column]) * scale
            total = term if total is None else total + term
        couplings.append(total)

    first = 3 - ((me >> (DEPTH - 1)) & 1)
    top_buf[0] = (nn_dot(lvl3[first], transfer_ref[DEPTH - 1, 0])
                  + nn_dot(lvl3[first + 1], transfer_ref[DEPTH - 1, 1]))
    top_copies = []
    for k in range(1, top_count):
        copy = pltpu.make_async_remote_copy(
            src_ref=top_buf.at[0], dst_ref=top_buf.at[k], send_sem=top_send.at[k - 1],
            recv_sem=top_recv.at[k - 1], device_id=((me + k * stride) % count,),
            device_id_type=MESH_ID)
        copy.start()
        top_copies.append(copy)
    for copy in top_copies:
        copy.wait()
    blended = top_buf[0] * weight_ref[0]
    for k in range(1, top_count):
        blended = blended + top_buf[k] * weight_ref[k]
    downward = nt_dot(blended, top_couple_ref[...])
    for level in reversed(range(DEPTH)):
        bit = (me >> level) & 1
        downward = couplings[level] + nt_dot(downward, transfer_ref[level, bit])
    down_out[...] = downward


def tree_exchange(node_t, coef_flat, lo, hi, transfer, couple, top_couple, links, weights, count):
    top_count = count >> DEPTH
    n_copies = 2 + 2 * REACH + 2 * NODE_REACH
    span = 1 << (DEPTH - 1)
    vectors, rank = node_t.shape
    vmem = pl.BlockSpec(memory_space=pltpu.VMEM)
    smem = pl.BlockSpec(memory_space=pltpu.SMEM)
    return pl.pallas_call(
        functools.partial(tree_kernel, count, top_count),
        out_shape=(
            jax.ShapeDtypeStruct(node_t.shape, jnp.float32),
            jax.ShapeDtypeStruct((2 * REACH + 1,) + coef_flat.shape, jnp.float32),
            jax.ShapeDtypeStruct((2,) + lo.shape, jnp.float32),
        ),
        in_specs=[vmem] * 7 + [smem, smem],
        out_specs=(vmem, vmem, vmem),
        scratch_shapes=[
            pltpu.VMEM((2 * NODE_REACH + 1,) + node_t.shape, jnp.float32),
            pltpu.VMEM((2 * REACH + 1,) + coef_flat.shape, jnp.float32),
            pltpu.VMEM((2,) + lo.shape, jnp.float32),
            pltpu.VMEM((top_count,) + node_t.shape, jnp.float32),
            pltpu.VMEM((7 * span // 2, vectors, rank), jnp.float32),
            pltpu.VMEM((7 * span // 4, vectors, rank), jnp.float32),
            pltpu.VMEM((7 * span // 8, vectors, rank), jnp.float32),
            pltpu.SemaphoreType.DMA((n_copies,)),
            pltpu.SemaphoreType.DMA((n_copies,)),
            pltpu.SemaphoreType.DMA((top_count - 1,)),
            pltpu.SemaphoreType.DMA((top_count - 1,)),
        ],
        compiler_params=pltpu.CompilerParams(collective_id=0, has_side_effects=True),
    )(node_t, coef_flat, lo, hi, transfer, couple, top_couple, links, weights)


def mat(m, x):
    return jnp.einsum("qr,rs->qs", m, x, precision=HIGHEST_PRECISION)


def up_pairs(transfer_level, nodes):
    paired = nodes.reshape(nodes.shape[0] // 2, 2, nodes.shape[1], nodes.shape[2])
    parent = jnp.einsum("rq,nrs->nqs", transfer_level[0], paired[:, 0], precision=HIGHEST_PRECISION)
    return parent + jnp.einsum("rq,nrs->nqs", transfer_level[1], paired[:, 1], precision=HIGHEST_PRECISION)


def local(
    points,
    order,
    bases,
    lift,
    near_ids,
    near_blocks,
    far_ids,
    far_count,
    far_blocks,
    transfer,
    couple,
    links,
    top_couple,
):
    position = lax.axis_index("leaf")
    count = lax.axis_size("leaf")
    vectors, points_dev = points.shape
    leaf_dev, leaf_size, rank_size = bases.shape
    local_order = order - position * points_dev
    tree_x = jnp.take(points, local_order, axis=1)
    blocks = tree_x.reshape(vectors, leaf_dev, leaf_size)
    leaf_coef = jnp.einsum("lpr,slp->lrs", bases, blocks, precision=HIGHEST_PRECISION)
    node_t = jnp.einsum("lrq,lrs->sq", lift, leaf_coef, precision=HIGHEST_PRECISION)
    top_count = count >> DEPTH
    top_index = position >> DEPTH
    ks = jnp.arange(top_count, dtype=jnp.int32)
    partner_index = (top_index - ks + top_count) % top_count
    distance = jnp.abs(partner_index - top_index)
    weights = jnp.where(distance >= 2, 1.0 / jnp.maximum(distance, 1).astype(jnp.float32), 0.0)
    down_t, coef_win, edges = tree_exchange(
        node_t,
        leaf_coef.reshape(-1, 128),
        tree_x[:, :leaf_size],
        tree_x[:, points_dev - leaf_size:],
        transfer, couple, top_couple, links[0], weights, count,
    )
    down_zero = down_t.T

    extended = jnp.concatenate([edges[0], tree_x, edges[1]], axis=1)
    extended = extended.reshape(vectors, leaf_dev + 2, leaf_size)
    near_local = near_ids - position * leaf_dev + 1
    gathered_near = jnp.take(extended, near_local, axis=1)
    near_part = jnp.einsum("lkpq,slkq->slp", near_blocks, gathered_near, precision=HIGHEST_PRECISION)
    window = coef_win.reshape((2 * REACH + 1) * leaf_dev, rank_size, vectors)
    window_slot = (far_ids // leaf_dev - position + REACH) * leaf_dev + far_ids % leaf_dev
    picked = jnp.take(window, window_slot, axis=0)
    active = (jnp.arange(far_ids.shape[1], dtype=jnp.int32)[None, :] < far_count[:, None]).astype(
        jnp.float32
    )
    picked = picked * active[:, :, None, None]
    far_part = jnp.einsum("lkrq,lkqs->lrs", far_blocks, picked, precision=HIGHEST_PRECISION)
    leaf_out = jnp.einsum("lrq,qs->lrs", lift, down_zero, precision=HIGHEST_PRECISION) + far_part
    tree_y = near_part + jnp.einsum("lpr,lrs->slp", bases, leaf_out, precision=HIGHEST_PRECISION)
    tree_y = tree_y.reshape(vectors, points_dev)
    return jnp.zeros((vectors, points_dev), jnp.float32).at[:, local_order].set(tree_y)


def solution(mesh):
    in_specs = (
        P(None, "leaf"),
        P("leaf"),
        P("leaf", None, None),
        P("leaf", None, None),
        P("leaf", None),
        P("leaf", None, None, None),
        P("leaf", None),
        P("leaf"),
        P("leaf", None, None, None),
        P(),
        P(),
        P("leaf", None, None),
        P(),
    )
    out_specs = P(None, "leaf")
    return jax.shard_map(local, mesh=mesh, in_specs=in_specs, out_specs=out_specs, check_vma=False)
```

```python
import functools

import jax
import jax.numpy as jnp
from jax import lax
from jax.experimental import pallas as pl
from jax.experimental.pallas import tpu as pltpu
from jax.sharding import PartitionSpec as P

REACH = 4
DEPTH = 4
NODE_REACH = 4 * (1 << (DEPTH - 1)) - 1

HIGHEST_PRECISION = lax.Precision.HIGHEST
OFFSETS = (-3, -2, 2, 3)
MESH_ID = pl.DeviceIdType.MESH


def nt_dot(x, y):
    return lax.dot_general(x, y, (((1,), (1,)), ((), ())), precision=HIGHEST_PRECISION,
                           preferred_element_type=jnp.float32)


def nn_dot(x, y):
    return jnp.dot(x, y, precision=HIGHEST_PRECISION, preferred_element_type=jnp.float32)


def up_level(nodes, t_even, t_odd):
    half, vectors, rank = nodes.shape[0] // 2, nodes.shape[1], nodes.shape[2]
    paired = nodes.reshape(half, 2 * vectors, rank)
    even = paired[:, :vectors].reshape(half * vectors, rank)
    odd = paired[:, vectors:].reshape(half * vectors, rank)
    return (nn_dot(even, t_even) + nn_dot(odd, t_odd)).reshape(half, vectors, rank)


def tree_kernel(count, top_count,
                node_ref, coef_ref, lo_ref, hi_ref, transfer_ref, couple_ref, top_couple_ref,
                links_ref, weight_ref,
                down_out, coef_out, edge_out,
                node_buf, coef_buf, edge_buf, top_buf, lvl1, lvl2, lvl3,
                send_sem, recv_sem, top_send, top_recv):
    me = lax.axis_index("leaf")
    stride = count // top_count
    barrier = pltpu.get_barrier_semaphore()
    targets = []
    for k in range(1, NODE_REACH + 1):
        targets += [(me + k) % count, (me + count - k) % count]
    for k in range(2, top_count - 1):
        if k * stride > NODE_REACH and count - k * stride > NODE_REACH:
            targets.append((me + k * stride) % count)
    for dest in targets:
        pl.semaphore_signal(barrier, inc=1, device_id=(dest,), device_id_type=MESH_ID)
    pl.semaphore_wait(barrier, len(targets))

    copies = []

    def push(src, dst, dest):
        index = len(copies)
        copy = pltpu.make_async_remote_copy(
            src_ref=src, dst_ref=dst, send_sem=send_sem.at[index],
            recv_sem=recv_sem.at[index], device_id=(dest,), device_id_type=MESH_ID)
        copy.start()
        copies.append(copy)
        return copy

    block = 1 << DEPTH
    near_nodes = []
    for k in range(1, block):
        near_nodes.append(push(node_ref, node_buf.at[NODE_REACH - k], (me + k) % count))
        near_nodes.append(push(node_ref, node_buf.at[NODE_REACH + k], (me + count - k) % count))
    rest = []
    for k in range(block, NODE_REACH + 1):
        rest.append(push(node_ref, node_buf.at[NODE_REACH - k], (me + k) % count))
        rest.append(push(node_ref, node_buf.at[NODE_REACH + k], (me + count - k) % count))
    for k in range(1, REACH + 1):
        rest.append(push(coef_ref, coef_buf.at[REACH - k], (me + k) % count))
        rest.append(push(coef_ref, coef_buf.at[REACH + k], (me + count - k) % count))
    rest.append(push(hi_ref, edge_buf.at[0], (me + 1) % count))
    rest.append(push(lo_ref, edge_buf.at[1], (me + count - 1) % count))
    node_buf[NODE_REACH] = node_ref[...]
    coef_buf[REACH] = coef_ref[...]
    for copy in near_nodes:
        copy.wait()

    own = node_buf[pl.ds(NODE_REACH - me % block, block)]
    for level in range(DEPTH):
        own = up_level(own, transfer_ref[level, 0], transfer_ref[level, 1])
    top_buf[0] = own[0]
    top_copies = []
    for k in range(1, top_count):
        copy = pltpu.make_async_remote_copy(
            src_ref=top_buf.at[0], dst_ref=top_buf.at[k], send_sem=top_send.at[k - 1],
            recv_sem=top_recv.at[k - 1], device_id=((me + k * stride) % count,),
            device_id_type=MESH_ID)
        copy.start()
        top_copies.append(copy)

    for copy in rest:
        copy.wait()
    coef_out[...] = coef_buf[...]
    edge_out[...] = edge_buf[...]

    span = 1 << (DEPTH - 1)
    low = me % span
    width = 7 * span
    start = NODE_REACH - 3 * span - low
    aligned = node_buf[pl.ds(start, width)]
    source = me - NODE_REACH + start + lax.broadcasted_iota(jnp.int32, aligned.shape, 0)
    aligned = jnp.where((source >= 0) & (source < count), aligned, 0.0)
    lvl1[...] = up_level(aligned, transfer_ref[0, 0], transfer_ref[0, 1])
    lvl2[...] = up_level(lvl1[...], transfer_ref[1, 0], transfer_ref[1, 1])
    lvl3[...] = up_level(lvl2[...], transfer_ref[2, 0], transfer_ref[2, 1])

    couplings = []
    for level in range(DEPTH):
        centre = (low >> level) + ((3 * span) >> level)
        total = None
        for column, offset in enumerate(OFFSETS):
            if level == 0:
                partner = node_buf[NODE_REACH + offset]
                inside = (me + offset >= 0) & (me + offset < count)
                partner = jnp.where(inside, partner, 0.0)
            else:
                partner = (lvl1, lvl2, lvl3)[level - 1][centre + offset]
            scale = links_ref[level, column].astype(jnp.float32)
            term = nt_dot(partner, couple_ref[level, column]) * scale
            total = term if total is None else total + term
        couplings.append(total)

    for copy in top_copies:
        copy.wait()
    blended = top_buf[0] * weight_ref[0]
    for k in range(1, top_count):
        blended = blended + top_buf[k] * weight_ref[k]
    downward = nt_dot(blended, top_couple_ref[...])
    for level in reversed(range(DEPTH)):
        bit = (me >> level) & 1
        downward = couplings[level] + nt_dot(downward, transfer_ref[level, bit])
    down_out[...] = downward


def tree_exchange(node_t, coef_flat, lo, hi, transfer, couple, top_couple, links, weights, count):
    top_count = count >> DEPTH
    n_copies = 2 + 2 * REACH + 2 * NODE_REACH
    span = 1 << (DEPTH - 1)
    vectors, rank = node_t.shape
    vmem = pl.BlockSpec(memory_space=pltpu.VMEM)
    smem = pl.BlockSpec(memory_space=pltpu.SMEM)
    return pl.pallas_call(
        functools.partial(tree_kernel, count, top_count),
        out_shape=(
            jax.ShapeDtypeStruct(node_t.shape, jnp.float32),
            jax.ShapeDtypeStruct((2 * REACH + 1,) + coef_flat.shape, jnp.float32),
            jax.ShapeDtypeStruct((2,) + lo.shape, jnp.float32),
        ),
        in_specs=[vmem] * 7 + [smem, smem],
        out_specs=(vmem, vmem, vmem),
        scratch_shapes=[
            pltpu.VMEM((2 * NODE_REACH + 1,) + node_t.shape, jnp.float32),
            pltpu.VMEM((2 * REACH + 1,) + coef_flat.shape, jnp.float32),
            pltpu.VMEM((2,) + lo.shape, jnp.float32),
            pltpu.VMEM((top_count,) + node_t.shape, jnp.float32),
            pltpu.VMEM((7 * span // 2, vectors, rank), jnp.float32),
            pltpu.VMEM((7 * span // 4, vectors, rank), jnp.float32),
            pltpu.VMEM((7 * span // 8, vectors, rank), jnp.float32),
            pltpu.SemaphoreType.DMA((n_copies,)),
            pltpu.SemaphoreType.DMA((n_copies,)),
            pltpu.SemaphoreType.DMA((top_count - 1,)),
            pltpu.SemaphoreType.DMA((top_count - 1,)),
        ],
        compiler_params=pltpu.CompilerParams(collective_id=0, has_side_effects=True),
    )(node_t, coef_flat, lo, hi, transfer, couple, top_couple, links, weights)


def mat(m, x):
    return jnp.einsum("qr,rs->qs", m, x, precision=HIGHEST_PRECISION)


def up_pairs(transfer_level, nodes):
    paired = nodes.reshape(nodes.shape[0] // 2, 2, nodes.shape[1], nodes.shape[2])
    parent = jnp.einsum("rq,nrs->nqs", transfer_level[0], paired[:, 0], precision=HIGHEST_PRECISION)
    return parent + jnp.einsum("rq,nrs->nqs", transfer_level[1], paired[:, 1], precision=HIGHEST_PRECISION)


def local(
    points,
    order,
    bases,
    lift,
    near_ids,
    near_blocks,
    far_ids,
    far_count,
    far_blocks,
    transfer,
    couple,
    links,
    top_couple,
):
    position = lax.axis_index("leaf")
    count = lax.axis_size("leaf")
    vectors, points_dev = points.shape
    leaf_dev, leaf_size, rank_size = bases.shape
    local_order = order - position * points_dev
    tree_x = jnp.take(points, local_order, axis=1)
    blocks = tree_x.reshape(vectors, leaf_dev, leaf_size)
    leaf_coef = jnp.einsum("lpr,slp->lrs", bases, blocks, precision=HIGHEST_PRECISION)
    node_t = jnp.einsum("lrq,lrs->sq", lift, leaf_coef, precision=HIGHEST_PRECISION)
    top_count = count >> DEPTH
    top_index = position >> DEPTH
    ks = jnp.arange(top_count, dtype=jnp.int32)
    partner_index = (top_index - ks + top_count) % top_count
    distance = jnp.abs(partner_index - top_index)
    weights = jnp.where(distance >= 2, 1.0 / jnp.maximum(distance, 1).astype(jnp.float32), 0.0)
    down_t, coef_win, edges = tree_exchange(
        node_t,
        leaf_coef.reshape(-1, 128),
        tree_x[:, :leaf_size],
        tree_x[:, points_dev - leaf_size:],
        transfer, couple, top_couple, links[0], weights, count,
    )
    down_zero = down_t.T

    extended = jnp.concatenate([edges[0], tree_x, edges[1]], axis=1)
    extended = extended.reshape(vectors, leaf_dev + 2, leaf_size)
    near_local = near_ids - position * leaf_dev + 1
    gathered_near = jnp.take(extended, near_local, axis=1)
    near_part = jnp.einsum("lkpq,slkq->slp", near_blocks, gathered_near, precision=HIGHEST_PRECISION)
    window = coef_win.reshape((2 * REACH + 1) * leaf_dev, rank_size, vectors)
    window_slot = (far_ids // leaf_dev - position + REACH) * leaf_dev + far_ids % leaf_dev
    picked = jnp.take(window, window_slot, axis=0)
    active = (jnp.arange(far_ids.shape[1], dtype=jnp.int32)[None, :] < far_count[:, None]).astype(
        jnp.float32
    )
    picked = picked * active[:, :, None, None]
    far_part = jnp.einsum("lkrq,lkqs->lrs", far_blocks, picked, precision=HIGHEST_PRECISION)
    leaf_out = jnp.einsum("lrq,qs->lrs", lift, down_zero, precision=HIGHEST_PRECISION) + far_part
    tree_y = near_part + jnp.einsum("lpr,lrs->slp", bases, leaf_out, precision=HIGHEST_PRECISION)
    tree_y = tree_y.reshape(vectors, points_dev)
    return jnp.zeros((vectors, points_dev), jnp.float32).at[:, local_order].set(tree_y)


def solution(mesh):
    in_specs = (
        P(None, "leaf"),
        P("leaf"),
        P("leaf", None, None),
        P("leaf", None, None),
        P("leaf", None),
        P("leaf", None, None, None),
        P("leaf", None),
        P("leaf"),
        P("leaf", None, None, None),
        P(),
        P(),
        P("leaf", None, None),
        P(),
    )
    out_specs = P(None, "leaf")
    return jax.shard_map(local, mesh=mesh, in_specs=in_specs, out_specs=out_specs, check_vma=False)
```

```python
import functools

import jax
import jax.numpy as jnp
from jax import lax
from jax.experimental import pallas as pl
from jax.experimental.pallas import tpu as pltpu
from jax.sharding import PartitionSpec as P

REACH = 4
DEPTH = 4
NODE_REACH = 4 * (1 << (DEPTH - 1)) - 1

HIGHEST_PRECISION = lax.Precision.HIGHEST
OFFSETS = (-3, -2, 2, 3)
MESH_ID = pl.DeviceIdType.MESH


def nt_dot(x, y):
    return lax.dot_general(x, y, (((1,), (1,)), ((), ())), precision=HIGHEST_PRECISION,
                           preferred_element_type=jnp.float32)


def nn_dot(x, y):
    return jnp.dot(x, y, precision=HIGHEST_PRECISION, preferred_element_type=jnp.float32)


def up_level(nodes, t_even, t_odd):
    half, vectors, rank = nodes.shape[0] // 2, nodes.shape[1], nodes.shape[2]
    paired = nodes.reshape(half, 2 * vectors, rank)
    even = paired[:, :vectors].reshape(half * vectors, rank)
    odd = paired[:, vectors:].reshape(half * vectors, rank)
    return (nn_dot(even, t_even) + nn_dot(odd, t_odd)).reshape(half, vectors, rank)


def tree_kernel(count, top_count,
                node_ref, coef_ref, x_ref, near_ref, transfer_ref, couple_ref, top_couple_ref,
                links_ref, weight_ref, slot_ref,
                down_out, coef_out, near_out,
                node_buf, coef_buf, ext_buf, top_buf, lvl1, lvl2, lvl3,
                send_sem, recv_sem, top_send, top_recv):
    me = lax.axis_index("leaf")
    stride = count // top_count
    barrier = pltpu.get_barrier_semaphore()
    targets = []
    for k in range(1, NODE_REACH + 1):
        targets += [(me + k) % count, (me + count - k) % count]
    for k in range(2, top_count - 1):
        if k * stride > NODE_REACH and count - k * stride > NODE_REACH:
            targets.append((me + k * stride) % count)
    for dest in targets:
        pl.semaphore_signal(barrier, inc=1, device_id=(dest,), device_id_type=MESH_ID)
    pl.semaphore_wait(barrier, len(targets))

    copies = []

    def push(src, dst, dest):
        index = len(copies)
        copy = pltpu.make_async_remote_copy(
            src_ref=src, dst_ref=dst, send_sem=send_sem.at[index],
            recv_sem=recv_sem.at[index], device_id=(dest,), device_id_type=MESH_ID)
        copy.start()
        copies.append(copy)
        return copy

    block = 1 << DEPTH
    near_nodes = []
    for k in range(1, block):
        near_nodes.append(push(node_ref, node_buf.at[NODE_REACH - k], (me + k) % count))
        near_nodes.append(push(node_ref, node_buf.at[NODE_REACH + k], (me + count - k) % count))
    rest = []
    for k in range(block, NODE_REACH + 1):
        rest.append(push(node_ref, node_buf.at[NODE_REACH - k], (me + k) % count))
        rest.append(push(node_ref, node_buf.at[NODE_REACH + k], (me + count - k) % count))
    for k in range(1, REACH + 1):
        rest.append(push(coef_ref, coef_buf.at[REACH - k], (me + k) % count))
        rest.append(push(coef_ref, coef_buf.at[REACH + k], (me + count - k) % count))
    leaves, leaf_size = ext_buf.shape[0] - 2, ext_buf.shape[2]
    rest.append(push(x_ref.at[:, pl.ds((leaves - 1) * leaf_size, leaf_size)], ext_buf.at[0],
                     (me + 1) % count))
    rest.append(push(x_ref.at[:, pl.ds(0, leaf_size)], ext_buf.at[leaves + 1],
                     (me + count - 1) % count))
    node_buf[NODE_REACH] = node_ref[...]
    coef_buf[REACH] = coef_ref[...]
    for copy in near_nodes:
        copy.wait()

    own = node_buf[pl.ds(NODE_REACH - me % block, block)]
    for level in range(DEPTH):
        own = up_level(own, transfer_ref[level, 0], transfer_ref[level, 1])
    top_buf[0] = own[0]
    top_copies = []
    for k in range(1, top_count):
        copy = pltpu.make_async_remote_copy(
            src_ref=top_buf.at[0], dst_ref=top_buf.at[k], send_sem=top_send.at[k - 1],
            recv_sem=top_recv.at[k - 1], device_id=((me + k * stride) % count,),
            device_id_type=MESH_ID)
        copy.start()
        top_copies.append(copy)

    for leaf in range(leaves):
        own_x = x_ref[:, pl.ds(leaf * leaf_size, leaf_size)]
        ext_buf[leaf + 1] = own_x
        near_out[:, pl.ds(leaf * leaf_size, leaf_size)] = nt_dot(own_x, near_ref[leaf, 0])

    for copy in rest:
        copy.wait()
    coef_out[...] = coef_buf[...]
    for leaf in range(leaves):
        total = near_out[:, pl.ds(leaf * leaf_size, leaf_size)]
        for column in range(1, near_ref.shape[1]):
            total = total + nt_dot(ext_buf[slot_ref[leaf, column]], near_ref[leaf, column])
        near_out[:, pl.ds(leaf * leaf_size, leaf_size)] = total

    span = 1 << (DEPTH - 1)
    low = me % span
    width = 7 * span
    start = NODE_REACH - 3 * span - low
    aligned = node_buf[pl.ds(start, width)]
    source = me - NODE_REACH + start + lax.broadcasted_iota(jnp.int32, aligned.shape, 0)
    aligned = jnp.where((source >= 0) & (source < count), aligned, 0.0)
    lvl1[...] = up_level(aligned, transfer_ref[0, 0], transfer_ref[0, 1])
    lvl2[...] = up_level(lvl1[...], transfer_ref[1, 0], transfer_ref[1, 1])
    lvl3[...] = up_level(lvl2[...], transfer_ref[2, 0], transfer_ref[2, 1])

    couplings = []
    for level in range(DEPTH):
        centre = (low >> level) + ((3 * span) >> level)
        total = None
        for column, offset in enumerate(OFFSETS):
            if level == 0:
                partner = node_buf[NODE_REACH + offset]
                inside = (me + offset >= 0) & (me + offset < count)
                partner = jnp.where(inside, partner, 0.0)
            else:
                partner = (lvl1, lvl2, lvl3)[level - 1][centre + offset]
            scale = links_ref[level, column].astype(jnp.float32)
            term = nt_dot(partner, couple_ref[level, column]) * scale
            total = term if total is None else total + term
        couplings.append(total)

    for copy in top_copies:
        copy.wait()
    blended = top_buf[0] * weight_ref[0]
    for k in range(1, top_count):
        blended = blended + top_buf[k] * weight_ref[k]
    downward = nt_dot(blended, top_couple_ref[...])
    for level in reversed(range(DEPTH)):
        bit = (me >> level) & 1
        downward = couplings[level] + nt_dot(downward, transfer_ref[level, bit])
    down_out[...] = downward


def tree_exchange(node_t, coef_flat, tree_x, near_blocks, transfer, couple, top_couple, links,
                  weights, near_slot, count):
    top_count = count >> DEPTH
    n_copies = 2 + 2 * REACH + 2 * NODE_REACH
    span = 1 << (DEPTH - 1)
    vectors, rank = node_t.shape
    leaves, leaf_size = near_blocks.shape[0], near_blocks.shape[2]
    vmem = pl.BlockSpec(memory_space=pltpu.VMEM)
    smem = pl.BlockSpec(memory_space=pltpu.SMEM)
    return pl.pallas_call(
        functools.partial(tree_kernel, count, top_count),
        out_shape=(
            jax.ShapeDtypeStruct(node_t.shape, jnp.float32),
            jax.ShapeDtypeStruct((2 * REACH + 1,) + coef_flat.shape, jnp.float32),
            jax.ShapeDtypeStruct(tree_x.shape, jnp.float32),
        ),
        in_specs=[vmem] * 7 + [smem, smem, smem],
        out_specs=(vmem, vmem, vmem),
        scratch_shapes=[
            pltpu.VMEM((2 * NODE_REACH + 1,) + node_t.shape, jnp.float32),
            pltpu.VMEM((2 * REACH + 1,) + coef_flat.shape, jnp.float32),
            pltpu.VMEM((leaves + 2, vectors, leaf_size), jnp.float32),
            pltpu.VMEM((top_count,) + node_t.shape, jnp.float32),
            pltpu.VMEM((7 * span // 2, vectors, rank), jnp.float32),
            pltpu.VMEM((7 * span // 4, vectors, rank), jnp.float32),
            pltpu.VMEM((7 * span // 8, vectors, rank), jnp.float32),
            pltpu.SemaphoreType.DMA((n_copies,)),
            pltpu.SemaphoreType.DMA((n_copies,)),
            pltpu.SemaphoreType.DMA((top_count - 1,)),
            pltpu.SemaphoreType.DMA((top_count - 1,)),
        ],
        compiler_params=pltpu.CompilerParams(collective_id=0, has_side_effects=True),
    )(node_t, coef_flat, tree_x, near_blocks, transfer, couple, top_couple, links, weights,
      near_slot)


def mat(m, x):
    return jnp.einsum("qr,rs->qs", m, x, precision=HIGHEST_PRECISION)


def up_pairs(transfer_level, nodes):
    paired = nodes.reshape(nodes.shape[0] // 2, 2, nodes.shape[1], nodes.shape[2])
    parent = jnp.einsum("rq,nrs->nqs", transfer_level[0], paired[:, 0], precision=HIGHEST_PRECISION)
    return parent + jnp.einsum("rq,nrs->nqs", transfer_level[1], paired[:, 1], precision=HIGHEST_PRECISION)


def local(
    points,
    order,
    bases,
    lift,
    near_ids,
    near_blocks,
    far_ids,
    far_count,
    far_blocks,
    transfer,
    couple,
    links,
    top_couple,
):
    position = lax.axis_index("leaf")
    count = lax.axis_size("leaf")
    vectors, points_dev = points.shape
    leaf_dev, leaf_size, rank_size = bases.shape
    local_order = order - position * points_dev
    tree_x = jnp.take(points, local_order, axis=1)
    blocks = tree_x.reshape(vectors, leaf_dev, leaf_size)
    leaf_coef = jnp.einsum("lpr,slp->lrs", bases, blocks, precision=HIGHEST_PRECISION)
    node_t = jnp.einsum("lrq,lrs->sq", lift, leaf_coef, precision=HIGHEST_PRECISION)
    top_count = count >> DEPTH
    top_index = position >> DEPTH
    ks = jnp.arange(top_count, dtype=jnp.int32)
    partner_index = (top_index - ks + top_count) % top_count
    distance = jnp.abs(partner_index - top_index)
    weights = jnp.where(distance >= 2, 1.0 / jnp.maximum(distance, 1).astype(jnp.float32), 0.0)
    near_slot = near_ids - position * leaf_dev + 1
    down_t, coef_win, near_t = tree_exchange(
        node_t, leaf_coef.reshape(-1, 128), tree_x, near_blocks,
        transfer, couple, top_couple, links[0], weights, near_slot, count,
    )
    down_zero = down_t.T

    window = coef_win.reshape((2 * REACH + 1) * leaf_dev, rank_size, vectors)
    window_slot = (far_ids // leaf_dev - position + REACH) * leaf_dev + far_ids % leaf_dev
    picked = jnp.take(window, window_slot, axis=0)
    active = (jnp.arange(far_ids.shape[1], dtype=jnp.int32)[None, :] < far_count[:, None]).astype(
        jnp.float32
    )
    picked = picked * active[:, :, None, None]
    far_part = jnp.einsum("lkrq,lkqs->lrs", far_blocks, picked, precision=HIGHEST_PRECISION)
    leaf_out = jnp.einsum("lrq,qs->lrs", lift, down_zero, precision=HIGHEST_PRECISION) + far_part
    tree_y = near_t + jnp.einsum(
        "lpr,lrs->slp", bases, leaf_out, precision=HIGHEST_PRECISION
    ).reshape(vectors, points_dev)
    return jnp.zeros((vectors, points_dev), jnp.float32).at[:, local_order].set(tree_y)


def solution(mesh):
    in_specs = (
        P(None, "leaf"),
        P("leaf"),
        P("leaf", None, None),
        P("leaf", None, None),
        P("leaf", None),
        P("leaf", None, None, None),
        P("leaf", None),
        P("leaf"),
        P("leaf", None, None, None),
        P(),
        P(),
        P("leaf", None, None),
        P(),
    )
    out_specs = P(None, "leaf")
    return jax.shard_map(local, mesh=mesh, in_specs=in_specs, out_specs=out_specs, check_vma=False)
```

```python
import functools

import jax
import jax.numpy as jnp
from jax import lax
from jax.experimental import pallas as pl
from jax.experimental.pallas import tpu as pltpu
from jax.sharding import PartitionSpec as P

REACH = 4
DEPTH = 4
NODE_REACH = 4 * (1 << (DEPTH - 1)) - 1

HIGHEST_PRECISION = lax.Precision.HIGHEST
OFFSETS = (-3, -2, 2, 3)
MESH_ID = pl.DeviceIdType.MESH


def nt_dot(x, y):
    return lax.dot_general(x, y, (((1,), (1,)), ((), ())), precision=HIGHEST_PRECISION,
                           preferred_element_type=jnp.float32)


def nn_dot(x, y):
    return jnp.dot(x, y, precision=HIGHEST_PRECISION, preferred_element_type=jnp.float32)


def up_level(nodes, t_even, t_odd):
    half, vectors, rank = nodes.shape[0] // 2, nodes.shape[1], nodes.shape[2]
    paired = nodes.reshape(half, 2 * vectors, rank)
    even = paired[:, :vectors].reshape(half * vectors, rank)
    odd = paired[:, vectors:].reshape(half * vectors, rank)
    return (nn_dot(even, t_even) + nn_dot(odd, t_odd)).reshape(half, vectors, rank)


def tree_kernel(count, top_count,
                node_ref, coef_ref, x_ref, near_ref, transfer_ref, couple_ref, top_couple_ref,
                lift_ref, bases_ref, far_ref,
                links_ref, weight_ref, slot_ref, far_slot_ref, active_ref,
                near_out,
                node_buf, coef_buf, ext_buf, top_buf, lvl1, lvl2, lvl3,
                send_sem, recv_sem, top_send, top_recv):
    me = lax.axis_index("leaf")
    stride = count // top_count
    barrier = pltpu.get_barrier_semaphore()
    targets = []
    for k in range(1, NODE_REACH + 1):
        targets += [(me + k) % count, (me + count - k) % count]
    for k in range(2, top_count - 1):
        if k * stride > NODE_REACH and count - k * stride > NODE_REACH:
            targets.append((me + k * stride) % count)
    for dest in targets:
        pl.semaphore_signal(barrier, inc=1, device_id=(dest,), device_id_type=MESH_ID)
    pl.semaphore_wait(barrier, len(targets))

    copies = []

    def push(src, dst, dest):
        index = len(copies)
        copy = pltpu.make_async_remote_copy(
            src_ref=src, dst_ref=dst, send_sem=send_sem.at[index],
            recv_sem=recv_sem.at[index], device_id=(dest,), device_id_type=MESH_ID)
        copy.start()
        copies.append(copy)
        return copy

    block = 1 << DEPTH
    leaf_dev = coef_ref.shape[0]
    near_nodes = []
    for k in range(1, block):
        near_nodes.append(push(node_ref, node_buf.at[NODE_REACH - k], (me + k) % count))
        near_nodes.append(push(node_ref, node_buf.at[NODE_REACH + k], (me + count - k) % count))
    rest = []
    for k in range(block, NODE_REACH + 1):
        rest.append(push(node_ref, node_buf.at[NODE_REACH - k], (me + k) % count))
        rest.append(push(node_ref, node_buf.at[NODE_REACH + k], (me + count - k) % count))
    for k in range(1, REACH + 1):
        rest.append(push(coef_ref, coef_buf.at[pl.ds((REACH - k) * leaf_dev, leaf_dev)],
                         (me + k) % count))
        rest.append(push(coef_ref, coef_buf.at[pl.ds((REACH + k) * leaf_dev, leaf_dev)],
                         (me + count - k) % count))
    leaves, leaf_size = ext_buf.shape[0] - 2, ext_buf.shape[2]
    rest.append(push(x_ref.at[:, pl.ds((leaves - 1) * leaf_size, leaf_size)], ext_buf.at[0],
                     (me + 1) % count))
    rest.append(push(x_ref.at[:, pl.ds(0, leaf_size)], ext_buf.at[leaves + 1],
                     (me + count - 1) % count))
    node_buf[NODE_REACH] = node_ref[...]
    coef_buf[pl.ds(REACH * leaf_dev, leaf_dev)] = coef_ref[...]
    for copy in near_nodes:
        copy.wait()

    own = node_buf[pl.ds(NODE_REACH - me % block, block)]
    for level in range(DEPTH):
        own = up_level(own, transfer_ref[level, 0], transfer_ref[level, 1])
    top_buf[0] = own[0]
    top_copies = []
    for k in range(1, top_count):
        copy = pltpu.make_async_remote_copy(
            src_ref=top_buf.at[0], dst_ref=top_buf.at[k], send_sem=top_send.at[k - 1],
            recv_sem=top_recv.at[k - 1], device_id=((me + k * stride) % count,),
            device_id_type=MESH_ID)
        copy.start()
        top_copies.append(copy)

    for leaf in range(leaves):
        own_x = x_ref[:, pl.ds(leaf * leaf_size, leaf_size)]
        ext_buf[leaf + 1] = own_x
        near_out[:, pl.ds(leaf * leaf_size, leaf_size)] = nt_dot(own_x, near_ref[leaf, 0])

    for copy in rest:
        copy.wait()
    far_parts = []
    for leaf in range(leaf_dev):
        total = None
        for column in range(far_ref.shape[1]):
            partner = coef_buf[far_slot_ref[leaf, column]] * active_ref[leaf, column]
            term = nt_dot(partner, far_ref[leaf, column])
            total = term if total is None else total + term
        far_parts.append(total)
    for leaf in range(leaves):
        total = near_out[:, pl.ds(leaf * leaf_size, leaf_size)]
        for column in range(1, near_ref.shape[1]):
            total = total + nt_dot(ext_buf[slot_ref[leaf, column]], near_ref[leaf, column])
        near_out[:, pl.ds(leaf * leaf_size, leaf_size)] = total

    span = 1 << (DEPTH - 1)
    low = me % span
    width = 7 * span
    start = NODE_REACH - 3 * span - low
    aligned = node_buf[pl.ds(start, width)]
    source = me - NODE_REACH + start + lax.broadcasted_iota(jnp.int32, aligned.shape, 0)
    aligned = jnp.where((source >= 0) & (source < count), aligned, 0.0)
    lvl1[...] = up_level(aligned, transfer_ref[0, 0], transfer_ref[0, 1])
    lvl2[...] = up_level(lvl1[...], transfer_ref[1, 0], transfer_ref[1, 1])
    lvl3[...] = up_level(lvl2[...], transfer_ref[2, 0], transfer_ref[2, 1])

    couplings = []
    for level in range(DEPTH):
        centre = (low >> level) + ((3 * span) >> level)
        total = None
        for column, offset in enumerate(OFFSETS):
            if level == 0:
                partner = node_buf[NODE_REACH + offset]
                inside = (me + offset >= 0) & (me + offset < count)
                partner = jnp.where(inside, partner, 0.0)
            else:
                partner = (lvl1, lvl2, lvl3)[level - 1][centre + offset]
            scale = links_ref[level, column].astype(jnp.float32)
            term = nt_dot(partner, couple_ref[level, column]) * scale
            total = term if total is None else total + term
        couplings.append(total)

    for copy in top_copies:
        copy.wait()
    blended = top_buf[0] * weight_ref[0]
    for k in range(1, top_count):
        blended = blended + top_buf[k] * weight_ref[k]
    downward = nt_dot(blended, top_couple_ref[...])
    for level in reversed(range(DEPTH)):
        bit = (me >> level) & 1
        downward = couplings[level] + nt_dot(downward, transfer_ref[level, bit])
    for leaf in range(leaf_dev):
        leaf_out = nt_dot(downward, lift_ref[leaf]) + far_parts[leaf]
        where = pl.ds(leaf * leaf_size, leaf_size)
        near_out[:, where] = near_out[:, where] + nt_dot(leaf_out, bases_ref[leaf])


def tree_exchange(node_t, coef_t, tree_x, near_blocks, transfer, couple, top_couple, lift, bases,
                  far_blocks, links, weights, near_slot, far_slot, active, count):
    top_count = count >> DEPTH
    n_copies = 2 + 2 * REACH + 2 * NODE_REACH
    span = 1 << (DEPTH - 1)
    vectors, rank = node_t.shape
    leaves, leaf_size = near_blocks.shape[0], near_blocks.shape[2]
    vmem = pl.BlockSpec(memory_space=pltpu.VMEM)
    smem = pl.BlockSpec(memory_space=pltpu.SMEM)
    return pl.pallas_call(
        functools.partial(tree_kernel, count, top_count),
        out_shape=jax.ShapeDtypeStruct(tree_x.shape, jnp.float32),
        in_specs=[vmem] * 10 + [smem] * 5,
        out_specs=vmem,
        scratch_shapes=[
            pltpu.VMEM((2 * NODE_REACH + 1,) + node_t.shape, jnp.float32),
            pltpu.VMEM(((2 * REACH + 1) * leaves,) + node_t.shape, jnp.float32),
            pltpu.VMEM((leaves + 2, vectors, leaf_size), jnp.float32),
            pltpu.VMEM((top_count,) + node_t.shape, jnp.float32),
            pltpu.VMEM((7 * span // 2, vectors, rank), jnp.float32),
            pltpu.VMEM((7 * span // 4, vectors, rank), jnp.float32),
            pltpu.VMEM((7 * span // 8, vectors, rank), jnp.float32),
            pltpu.SemaphoreType.DMA((n_copies,)),
            pltpu.SemaphoreType.DMA((n_copies,)),
            pltpu.SemaphoreType.DMA((top_count - 1,)),
            pltpu.SemaphoreType.DMA((top_count - 1,)),
        ],
        compiler_params=pltpu.CompilerParams(collective_id=0, has_side_effects=True),
    )(node_t, coef_t, tree_x, near_blocks, transfer, couple, top_couple, lift, bases, far_blocks,
      links, weights, near_slot, far_slot, active)


def mat(m, x):
    return jnp.einsum("qr,rs->qs", m, x, precision=HIGHEST_PRECISION)


def up_pairs(transfer_level, nodes):
    paired = nodes.reshape(nodes.shape[0] // 2, 2, nodes.shape[1], nodes.shape[2])
    parent = jnp.einsum("rq,nrs->nqs", transfer_level[0], paired[:, 0], precision=HIGHEST_PRECISION)
    return parent + jnp.einsum("rq,nrs->nqs", transfer_level[1], paired[:, 1], precision=HIGHEST_PRECISION)


def local(
    points,
    order,
    bases,
    lift,
    near_ids,
    near_blocks,
    far_ids,
    far_count,
    far_blocks,
    transfer,
    couple,
    links,
    top_couple,
):
    position = lax.axis_index("leaf")
    count = lax.axis_size("leaf")
    vectors, points_dev = points.shape
    leaf_dev, leaf_size, rank_size = bases.shape
    local_order = order - position * points_dev
    tree_x = jnp.take(points, local_order, axis=1)
    blocks = tree_x.reshape(vectors, leaf_dev, leaf_size)
    coef_t = jnp.einsum("lpr,slp->lsr", bases, blocks, precision=HIGHEST_PRECISION)
    node_t = jnp.einsum("lrq,lsr->sq", lift, coef_t, precision=HIGHEST_PRECISION)
    top_count = count >> DEPTH
    top_index = position >> DEPTH
    ks = jnp.arange(top_count, dtype=jnp.int32)
    partner_index = (top_index - ks + top_count) % top_count
    distance = jnp.abs(partner_index - top_index)
    weights = jnp.where(distance >= 2, 1.0 / jnp.maximum(distance, 1).astype(jnp.float32), 0.0)
    near_slot = jnp.clip(near_ids - position * leaf_dev + 1, 0, leaf_dev + 1)
    far_slot = (far_ids // leaf_dev - position + REACH) * leaf_dev + far_ids % leaf_dev
    far_slot = jnp.clip(far_slot, 0, (2 * REACH + 1) * leaf_dev - 1)
    active = (jnp.arange(far_ids.shape[1], dtype=jnp.int32)[None, :] < far_count[:, None]).astype(
        jnp.float32
    )
    tree_y = tree_exchange(
        node_t, coef_t, tree_x, near_blocks, transfer, couple, top_couple, lift, bases,
        far_blocks, links[0], weights, near_slot, far_slot, active, count,
    )
    return jnp.zeros((vectors, points_dev), jnp.float32).at[:, local_order].set(tree_y)


def solution(mesh):
    in_specs = (
        P(None, "leaf"),
        P("leaf"),
        P("leaf", None, None),
        P("leaf", None, None),
        P("leaf", None),
        P("leaf", None, None, None),
        P("leaf", None),
        P("leaf"),
        P("leaf", None, None, None),
        P(),
        P(),
        P("leaf", None, None),
        P(),
    )
    out_specs = P(None, "leaf")
    return jax.shard_map(local, mesh=mesh, in_specs=in_specs, out_specs=out_specs, check_vma=False)
```

```python
import functools

import jax
import jax.numpy as jnp
from jax import lax
from jax.experimental import pallas as pl
from jax.experimental.pallas import tpu as pltpu
from jax.sharding import PartitionSpec as P

REACH = 4
DEPTH = 4
NODE_REACH = 4 * (1 << (DEPTH - 1)) - 1

HIGHEST_PRECISION = lax.Precision.HIGHEST
OFFSETS = (-3, -2, 2, 3)
MESH_ID = pl.DeviceIdType.MESH


def nt_dot(x, y):
    return lax.dot_general(x, y, (((1,), (1,)), ((), ())), precision=HIGHEST_PRECISION,
                           preferred_element_type=jnp.float32)


def nn_dot(x, y):
    return jnp.dot(x, y, precision=HIGHEST_PRECISION, preferred_element_type=jnp.float32)


def up_level(nodes, t_even, t_odd):
    half, vectors, rank = nodes.shape[0] // 2, nodes.shape[1], nodes.shape[2]
    paired = nodes.reshape(half, 2 * vectors, rank)
    even = paired[:, :vectors].reshape(half * vectors, rank)
    odd = paired[:, vectors:].reshape(half * vectors, rank)
    return (nn_dot(even, t_even) + nn_dot(odd, t_odd)).reshape(half, vectors, rank)


def tree_kernel(count, top_count,
                node_ref, coef_ref, x_ref, near_ref, transfer_ref, couple_ref, top_couple_ref,
                lift_ref, bases_ref, far_ref,
                links_ref, weight_ref, near_ids_ref, far_ids_ref, far_count_ref,
                near_out,
                node_buf, coef_buf, ext_buf, top_buf, lvl1, lvl2, lvl3,
                send_sem, recv_sem, top_send, top_recv):
    me = lax.axis_index("leaf")
    stride = count // top_count
    barrier = pltpu.get_barrier_semaphore()
    targets = []
    for k in range(1, NODE_REACH + 1):
        targets += [(me + k) % count, (me + count - k) % count]
    for k in range(2, top_count - 1):
        if k * stride > NODE_REACH and count - k * stride > NODE_REACH:
            targets.append((me + k * stride) % count)
    for dest in targets:
        pl.semaphore_signal(barrier, inc=1, device_id=(dest,), device_id_type=MESH_ID)
    pl.semaphore_wait(barrier, len(targets))

    copies = []

    def push(src, dst, dest):
        index = len(copies)
        copy = pltpu.make_async_remote_copy(
            src_ref=src, dst_ref=dst, send_sem=send_sem.at[index],
            recv_sem=recv_sem.at[index], device_id=(dest,), device_id_type=MESH_ID)
        copy.start()
        copies.append(copy)
        return copy

    block = 1 << DEPTH
    leaf_dev = coef_ref.shape[0]
    near_nodes = []
    for k in range(1, block):
        near_nodes.append(push(node_ref, node_buf.at[NODE_REACH - k], (me + k) % count))
        near_nodes.append(push(node_ref, node_buf.at[NODE_REACH + k], (me + count - k) % count))
    rest = []
    for k in range(block, NODE_REACH + 1):
        rest.append(push(node_ref, node_buf.at[NODE_REACH - k], (me + k) % count))
        rest.append(push(node_ref, node_buf.at[NODE_REACH + k], (me + count - k) % count))
    for k in range(1, REACH + 1):
        rest.append(push(coef_ref, coef_buf.at[pl.ds((REACH - k) * leaf_dev, leaf_dev)],
                         (me + k) % count))
        rest.append(push(coef_ref, coef_buf.at[pl.ds((REACH + k) * leaf_dev, leaf_dev)],
                         (me + count - k) % count))
    leaves, leaf_size = ext_buf.shape[0] - 2, ext_buf.shape[2]
    rest.append(push(x_ref.at[:, pl.ds((leaves - 1) * leaf_size, leaf_size)], ext_buf.at[0],
                     (me + 1) % count))
    rest.append(push(x_ref.at[:, pl.ds(0, leaf_size)], ext_buf.at[leaves + 1],
                     (me + count - 1) % count))
    node_buf[NODE_REACH] = node_ref[...]
    coef_buf[pl.ds(REACH * leaf_dev, leaf_dev)] = coef_ref[...]
    for copy in near_nodes:
        copy.wait()

    own = node_buf[pl.ds(NODE_REACH - me % block, block)]
    for level in range(DEPTH):
        own = up_level(own, transfer_ref[level, 0], transfer_ref[level, 1])
    top_buf[0] = own[0]
    top_copies = []
    for k in range(1, top_count):
        copy = pltpu.make_async_remote_copy(
            src_ref=top_buf.at[0], dst_ref=top_buf.at[k], send_sem=top_send.at[k - 1],
            recv_sem=top_recv.at[k - 1], device_id=((me + k * stride) % count,),
            device_id_type=MESH_ID)
        copy.start()
        top_copies.append(copy)

    for leaf in range(leaves):
        own_x = x_ref[:, pl.ds(leaf * leaf_size, leaf_size)]
        ext_buf[leaf + 1] = own_x
        near_out[:, pl.ds(leaf * leaf_size, leaf_size)] = nt_dot(own_x, near_ref[leaf, 0])

    for copy in rest:
        copy.wait()
    far_parts = []
    for leaf in range(leaf_dev):
        total = None
        for column in range(far_ref.shape[1]):
            far_id = far_ids_ref[leaf, column]
            slot = (far_id // leaf_dev - me + REACH) * leaf_dev + far_id % leaf_dev
            slot = jnp.minimum(jnp.maximum(slot, 0), (2 * REACH + 1) * leaf_dev - 1)
            scale = jnp.where(column < far_count_ref[leaf], 1.0, 0.0).astype(jnp.float32)
            partner = coef_buf[slot] * scale
            term = nt_dot(partner, far_ref[leaf, column])
            total = term if total is None else total + term
        far_parts.append(total)
    for leaf in range(leaves):
        total = near_out[:, pl.ds(leaf * leaf_size, leaf_size)]
        for column in range(1, near_ref.shape[1]):
            slot = near_ids_ref[column, leaf] - me * leaves + 1
            slot = jnp.minimum(jnp.maximum(slot, 0), leaves + 1)
            total = total + nt_dot(ext_buf[slot], near_ref[leaf, column])
        near_out[:, pl.ds(leaf * leaf_size, leaf_size)] = total

    span = 1 << (DEPTH - 1)
    low = me % span
    width = 7 * span
    start = NODE_REACH - 3 * span - low
    aligned = node_buf[pl.ds(start, width)]
    source = me - NODE_REACH + start + lax.broadcasted_iota(jnp.int32, aligned.shape, 0)
    aligned = jnp.where((source >= 0) & (source < count), aligned, 0.0)
    lvl1[...] = up_level(aligned, transfer_ref[0, 0], transfer_ref[0, 1])
    lvl2[...] = up_level(lvl1[...], transfer_ref[1, 0], transfer_ref[1, 1])
    lvl3[...] = up_level(lvl2[...], transfer_ref[2, 0], transfer_ref[2, 1])

    couplings = []
    for level in range(DEPTH):
        centre = (low >> level) + ((3 * span) >> level)
        total = None
        for column, offset in enumerate(OFFSETS):
            if level == 0:
                partner = node_buf[NODE_REACH + offset]
                inside = (me + offset >= 0) & (me + offset < count)
                partner = jnp.where(inside, partner, 0.0)
            else:
                partner = (lvl1, lvl2, lvl3)[level - 1][centre + offset]
            scale = links_ref[level, column].astype(jnp.float32)
            term = nt_dot(partner, couple_ref[level, column]) * scale
            total = term if total is None else total + term
        couplings.append(total)

    for copy in top_copies:
        copy.wait()
    blended = top_buf[0] * weight_ref[0]
    for k in range(1, top_count):
        blended = blended + top_buf[k] * weight_ref[k]
    downward = nt_dot(blended, top_couple_ref[...])
    for level in reversed(range(DEPTH)):
        bit = (me >> level) & 1
        downward = couplings[level] + nt_dot(downward, transfer_ref[level, bit])
    for leaf in range(leaf_dev):
        leaf_out = nt_dot(downward, lift_ref[leaf]) + far_parts[leaf]
        where = pl.ds(leaf * leaf_size, leaf_size)
        near_out[:, where] = near_out[:, where] + nn_dot(leaf_out, bases_ref[leaf])


def tree_exchange(node_t, coef_t, tree_x, near_blocks, transfer, couple, top_couple, lift, bases,
                  far_blocks, links, weights, near_ids, far_ids, far_count, count):
    top_count = count >> DEPTH
    n_copies = 2 + 2 * REACH + 2 * NODE_REACH
    span = 1 << (DEPTH - 1)
    vectors, rank = node_t.shape
    leaves, leaf_size = near_blocks.shape[0], near_blocks.shape[2]
    vmem = pl.BlockSpec(memory_space=pltpu.VMEM)
    smem = pl.BlockSpec(memory_space=pltpu.SMEM)
    return pl.pallas_call(
        functools.partial(tree_kernel, count, top_count),
        out_shape=jax.ShapeDtypeStruct(tree_x.shape, jnp.float32),
        in_specs=[vmem] * 10 + [smem] * 5,
        out_specs=vmem,
        scratch_shapes=[
            pltpu.VMEM((2 * NODE_REACH + 1,) + node_t.shape, jnp.float32),
            pltpu.VMEM(((2 * REACH + 1) * leaves,) + node_t.shape, jnp.float32),
            pltpu.VMEM((leaves + 2, vectors, leaf_size), jnp.float32),
            pltpu.VMEM((top_count,) + node_t.shape, jnp.float32),
            pltpu.VMEM((7 * span // 2, vectors, rank), jnp.float32),
            pltpu.VMEM((7 * span // 4, vectors, rank), jnp.float32),
            pltpu.VMEM((7 * span // 8, vectors, rank), jnp.float32),
            pltpu.SemaphoreType.DMA((n_copies,)),
            pltpu.SemaphoreType.DMA((n_copies,)),
            pltpu.SemaphoreType.DMA((top_count - 1,)),
            pltpu.SemaphoreType.DMA((top_count - 1,)),
        ],
        compiler_params=pltpu.CompilerParams(collective_id=0, has_side_effects=True),
    )(node_t, coef_t, tree_x, near_blocks, transfer, couple, top_couple, lift, bases, far_blocks,
      links, weights, near_ids, far_ids, far_count)


def mat(m, x):
    return jnp.einsum("qr,rs->qs", m, x, precision=HIGHEST_PRECISION)


def up_pairs(transfer_level, nodes):
    paired = nodes.reshape(nodes.shape[0] // 2, 2, nodes.shape[1], nodes.shape[2])
    parent = jnp.einsum("rq,nrs->nqs", transfer_level[0], paired[:, 0], precision=HIGHEST_PRECISION)
    return parent + jnp.einsum("rq,nrs->nqs", transfer_level[1], paired[:, 1], precision=HIGHEST_PRECISION)


def local(
    points,
    order,
    bases,
    lift,
    near_ids,
    near_blocks,
    far_ids,
    far_count,
    far_blocks,
    transfer,
    couple,
    links,
    top_couple,
):
    position = lax.axis_index("leaf")
    count = lax.axis_size("leaf")
    vectors, points_dev = points.shape
    leaf_dev, leaf_size, rank_size = bases.shape
    local_order = order - position * points_dev
    tree_x = jnp.take(points, local_order, axis=1, mode="clip")
    blocks = tree_x.reshape(vectors, leaf_dev, leaf_size)
    coef_t = jnp.einsum("lpr,slp->lsr", bases, blocks, precision=HIGHEST_PRECISION)
    node_t = jnp.einsum("lrq,lsr->sq", lift, coef_t, precision=HIGHEST_PRECISION)
    top_count = count >> DEPTH
    top_index = position >> DEPTH
    ks = jnp.arange(top_count, dtype=jnp.int32)
    partner_index = (top_index - ks + top_count) % top_count
    distance = jnp.abs(partner_index - top_index)
    weights = jnp.where(distance >= 2, 1.0 / jnp.maximum(distance, 1).astype(jnp.float32), 0.0)
    tree_y = tree_exchange(
        node_t, coef_t, tree_x, near_blocks, transfer, couple, top_couple, lift,
        jnp.swapaxes(bases, 1, 2), far_blocks, links[0], weights, near_ids.T, far_ids, far_count,
        count,
    )
    return jnp.zeros((vectors, points_dev), jnp.float32).at[:, local_order].set(tree_y, mode="clip")


def solution(mesh):
    in_specs = (
        P(None, "leaf"),
        P("leaf"),
        P("leaf", None, None),
        P("leaf", None, None),
        P("leaf", None),
        P("leaf", None, None, None),
        P("leaf", None),
        P("leaf"),
        P("leaf", None, None, None),
        P(),
        P(),
        P("leaf", None, None),
        P(),
    )
    out_specs = P(None, "leaf")
    return jax.shard_map(local, mesh=mesh, in_specs=in_specs, out_specs=out_specs, check_vma=False)
```

```python
import functools

import jax
import jax.numpy as jnp
from jax import lax
from jax.experimental import pallas as pl
from jax.experimental.pallas import tpu as pltpu
from jax.sharding import PartitionSpec as P

REACH = 4
DEPTH = 4
NODE_REACH = (1 << DEPTH) - 1

HIGHEST_PRECISION = lax.Precision.HIGHEST
OFFSETS = (-3, -2, 2, 3)
MESH_ID = pl.DeviceIdType.MESH


def nt_dot(x, y):
    return lax.dot_general(x, y, (((1,), (1,)), ((), ())), precision=HIGHEST_PRECISION,
                           preferred_element_type=jnp.float32)


def nn_dot(x, y):
    return jnp.dot(x, y, precision=HIGHEST_PRECISION, preferred_element_type=jnp.float32)


def up_level(nodes, t_even, t_odd):
    half, vectors, rank = nodes.shape[0] // 2, nodes.shape[1], nodes.shape[2]
    paired = nodes.reshape(half, 2 * vectors, rank)
    even = paired[:, :vectors].reshape(half * vectors, rank)
    odd = paired[:, vectors:].reshape(half * vectors, rank)
    return (nn_dot(even, t_even) + nn_dot(odd, t_odd)).reshape(half, vectors, rank)


def tree_kernel(count, top_count,
                node_ref, coef_ref, x_ref, near_ref, transfer_ref, couple_ref, top_couple_ref,
                lift_ref, bases_ref, far_ref,
                links_ref, weight_ref, near_ids_ref, far_ids_ref, far_count_ref,
                near_out,
                node_buf, coef_buf, ext_buf, top_buf, lvl1, lvl2, own3, far3,
                send_sem, recv_sem, top_send, top_recv, third_send, third_recv):
    me = lax.axis_index("leaf")
    stride = count // top_count
    barrier = pltpu.get_barrier_semaphore()
    targets = []
    for k in range(1, NODE_REACH + 1):
        targets += [(me + k) % count, (me + count - k) % count]
    block3 = 1 << (DEPTH - 1)
    for offset in OFFSETS:
        targets.append((me + count - offset * block3) % count)
    for k in range(2, top_count - 1):
        targets.append((me + k * stride) % count)
    for dest in targets:
        pl.semaphore_signal(barrier, inc=1, device_id=(dest,), device_id_type=MESH_ID)
    pl.semaphore_wait(barrier, len(targets))

    copies = []

    def push(src, dst, dest):
        index = len(copies)
        copy = pltpu.make_async_remote_copy(
            src_ref=src, dst_ref=dst, send_sem=send_sem.at[index],
            recv_sem=recv_sem.at[index], device_id=(dest,), device_id_type=MESH_ID)
        copy.start()
        copies.append(copy)
        return copy

    block = 1 << DEPTH
    leaf_dev = coef_ref.shape[0]
    near_nodes = []
    for k in range(1, block):
        near_nodes.append(push(node_ref, node_buf.at[NODE_REACH - k], (me + k) % count))
        near_nodes.append(push(node_ref, node_buf.at[NODE_REACH + k], (me + count - k) % count))
    rest = []
    for k in range(1, REACH + 1):
        rest.append(push(coef_ref, coef_buf.at[pl.ds((REACH - k) * leaf_dev, leaf_dev)],
                         (me + k) % count))
        rest.append(push(coef_ref, coef_buf.at[pl.ds((REACH + k) * leaf_dev, leaf_dev)],
                         (me + count - k) % count))
    leaves, leaf_size = ext_buf.shape[0] - 2, ext_buf.shape[2]
    rest.append(push(x_ref.at[:, pl.ds((leaves - 1) * leaf_size, leaf_size)], ext_buf.at[0],
                     (me + 1) % count))
    rest.append(push(x_ref.at[:, pl.ds(0, leaf_size)], ext_buf.at[leaves + 1],
                     (me + count - 1) % count))
    node_buf[NODE_REACH] = node_ref[...]
    coef_buf[pl.ds(REACH * leaf_dev, leaf_dev)] = coef_ref[...]
    for copy in near_nodes:
        copy.wait()

    own = node_buf[pl.ds(NODE_REACH - me % block, block)]
    for level in range(DEPTH - 1):
        own = up_level(own, transfer_ref[level, 0], transfer_ref[level, 1])
    own3[...] = own
    top_buf[0] = up_level(own, transfer_ref[DEPTH - 1, 0], transfer_ref[DEPTH - 1, 1])[0]
    mine3 = own3.at[(me >> (DEPTH - 1)) & 1]
    third = []
    for column, offset in enumerate(OFFSETS):
        copy = pltpu.make_async_remote_copy(
            src_ref=mine3, dst_ref=far3.at[column], send_sem=third_send.at[column],
            recv_sem=third_recv.at[column], device_id=((me + count - offset * block3) % count,),
            device_id_type=MESH_ID)
        copy.start()
        third.append(copy)
    top_copies = []
    for k in range(1, top_count):
        copy = pltpu.make_async_remote_copy(
            src_ref=top_buf.at[0], dst_ref=top_buf.at[k], send_sem=top_send.at[k - 1],
            recv_sem=top_recv.at[k - 1], device_id=((me + k * stride) % count,),
            device_id_type=MESH_ID)
        copy.start()
        top_copies.append(copy)

    for leaf in range(leaves):
        own_x = x_ref[:, pl.ds(leaf * leaf_size, leaf_size)]
        ext_buf[leaf + 1] = own_x
        near_out[:, pl.ds(leaf * leaf_size, leaf_size)] = nt_dot(own_x, near_ref[leaf, 0])

    for copy in rest:
        copy.wait()
    far_parts = []
    for leaf in range(leaf_dev):
        total = None
        for column in range(far_ref.shape[1]):
            far_id = far_ids_ref[leaf, column]
            slot = (far_id // leaf_dev - me + REACH) * leaf_dev + far_id % leaf_dev
            slot = jnp.minimum(jnp.maximum(slot, 0), (2 * REACH + 1) * leaf_dev - 1)
            scale = jnp.where(column < far_count_ref[leaf], 1.0, 0.0).astype(jnp.float32)
            partner = coef_buf[slot] * scale
            term = nt_dot(partner, far_ref[leaf, column])
            total = term if total is None else total + term
        far_parts.append(total)
    for leaf in range(leaves):
        total = near_out[:, pl.ds(leaf * leaf_size, leaf_size)]
        for column in range(1, near_ref.shape[1]):
            slot = near_ids_ref[column, leaf] - me * leaves + 1
            slot = jnp.minimum(jnp.maximum(slot, 0), leaves + 1)
            total = total + nt_dot(ext_buf[slot], near_ref[leaf, column])
        near_out[:, pl.ds(leaf * leaf_size, leaf_size)] = total

    span = 1 << (DEPTH - 2)
    low = me % span
    width = 7 * span
    start = NODE_REACH - 3 * span - low
    aligned = node_buf[pl.ds(start, width)]
    source = me - NODE_REACH + start + lax.broadcasted_iota(jnp.int32, aligned.shape, 0)
    aligned = jnp.where((source >= 0) & (source < count), aligned, 0.0)
    lvl1[...] = up_level(aligned, transfer_ref[0, 0], transfer_ref[0, 1])
    lvl2[...] = up_level(lvl1[...], transfer_ref[1, 0], transfer_ref[1, 1])
    for copy in third:
        copy.wait()

    couplings = []
    for level in range(DEPTH):
        centre = (low >> level) + ((3 * span) >> level)
        total = None
        for column, offset in enumerate(OFFSETS):
            if level == 0:
                partner = node_buf[NODE_REACH + offset]
                inside = (me + offset >= 0) & (me + offset < count)
                partner = jnp.where(inside, partner, 0.0)
            elif level == DEPTH - 1:
                partner = far3[column]
                inside = (me + offset * block3 >= 0) & (me + offset * block3 < count)
                partner = jnp.where(inside, partner, 0.0)
            else:
                partner = (lvl1, lvl2)[level - 1][centre + offset]
            scale = links_ref[level, column].astype(jnp.float32)
            term = nt_dot(partner, couple_ref[level, column]) * scale
            total = term if total is None else total + term
        couplings.append(total)

    for copy in top_copies:
        copy.wait()
    blended = top_buf[0] * weight_ref[0]
    for k in range(1, top_count):
        blended = blended + top_buf[k] * weight_ref[k]
    downward = nt_dot(blended, top_couple_ref[...])
    for level in reversed(range(DEPTH)):
        bit = (me >> level) & 1
        downward = couplings[level] + nt_dot(downward, transfer_ref[level, bit])
    for leaf in range(leaf_dev):
        leaf_out = nt_dot(downward, lift_ref[leaf]) + far_parts[leaf]
        where = pl.ds(leaf * leaf_size, leaf_size)
        near_out[:, where] = near_out[:, where] + nn_dot(leaf_out, bases_ref[leaf])


def tree_exchange(node_t, coef_t, tree_x, near_blocks, transfer, couple, top_couple, lift, bases,
                  far_blocks, links, weights, near_ids, far_ids, far_count, count):
    top_count = count >> DEPTH
    n_copies = 2 + 2 * REACH + 2 * NODE_REACH
    span = 1 << (DEPTH - 2)
    vectors, rank = node_t.shape
    leaves, leaf_size = near_blocks.shape[0], near_blocks.shape[2]
    vmem = pl.BlockSpec(memory_space=pltpu.VMEM)
    smem = pl.BlockSpec(memory_space=pltpu.SMEM)
    return pl.pallas_call(
        functools.partial(tree_kernel, count, top_count),
        out_shape=jax.ShapeDtypeStruct(tree_x.shape, jnp.float32),
        in_specs=[vmem] * 10 + [smem] * 5,
        out_specs=vmem,
        scratch_shapes=[
            pltpu.VMEM((2 * NODE_REACH + 1,) + node_t.shape, jnp.float32),
            pltpu.VMEM(((2 * REACH + 1) * leaves,) + node_t.shape, jnp.float32),
            pltpu.VMEM((leaves + 2, vectors, leaf_size), jnp.float32),
            pltpu.VMEM((top_count,) + node_t.shape, jnp.float32),
            pltpu.VMEM((7 * span // 2, vectors, rank), jnp.float32),
            pltpu.VMEM((7 * span // 4, vectors, rank), jnp.float32),
            pltpu.VMEM((2, vectors, rank), jnp.float32),
            pltpu.VMEM((len(OFFSETS), vectors, rank), jnp.float32),
            pltpu.SemaphoreType.DMA((n_copies,)),
            pltpu.SemaphoreType.DMA((n_copies,)),
            pltpu.SemaphoreType.DMA((top_count - 1,)),
            pltpu.SemaphoreType.DMA((top_count - 1,)),
            pltpu.SemaphoreType.DMA((len(OFFSETS),)),
            pltpu.SemaphoreType.DMA((len(OFFSETS),)),
        ],
        compiler_params=pltpu.CompilerParams(collective_id=0, has_side_effects=True),
    )(node_t, coef_t, tree_x, near_blocks, transfer, couple, top_couple, lift, bases, far_blocks,
      links, weights, near_ids, far_ids, far_count)


def mat(m, x):
    return jnp.einsum("qr,rs->qs", m, x, precision=HIGHEST_PRECISION)


def up_pairs(transfer_level, nodes):
    paired = nodes.reshape(nodes.shape[0] // 2, 2, nodes.shape[1], nodes.shape[2])
    parent = jnp.einsum("rq,nrs->nqs", transfer_level[0], paired[:, 0], precision=HIGHEST_PRECISION)
    return parent + jnp.einsum("rq,nrs->nqs", transfer_level[1], paired[:, 1], precision=HIGHEST_PRECISION)


def local(
    points,
    order,
    bases,
    lift,
    near_ids,
    near_blocks,
    far_ids,
    far_count,
    far_blocks,
    transfer,
    couple,
    links,
    top_couple,
):
    position = lax.axis_index("leaf")
    count = lax.axis_size("leaf")
    vectors, points_dev = points.shape
    leaf_dev, leaf_size, rank_size = bases.shape
    local_order = order - position * points_dev
    tree_x = jnp.take(points, local_order, axis=1, mode="clip")
    blocks = tree_x.reshape(vectors, leaf_dev, leaf_size)
    coef_t = jnp.einsum("lpr,slp->lsr", bases, blocks, precision=HIGHEST_PRECISION)
    node_t = jnp.einsum("lrq,lsr->sq", lift, coef_t, precision=HIGHEST_PRECISION)
    top_count = count >> DEPTH
    top_index = position >> DEPTH
    ks = jnp.arange(top_count, dtype=jnp.int32)
    partner_index = (top_index - ks + top_count) % top_count
    distance = jnp.abs(partner_index - top_index)
    weights = jnp.where(distance >= 2, 1.0 / jnp.maximum(distance, 1).astype(jnp.float32), 0.0)
    tree_y = tree_exchange(
        node_t, coef_t, tree_x, near_blocks, transfer, couple, top_couple, lift,
        jnp.swapaxes(bases, 1, 2), far_blocks, links[0], weights, near_ids.T, far_ids, far_count,
        count,
    )
    return jnp.zeros((vectors, points_dev), jnp.float32).at[:, local_order].set(tree_y, mode="clip")


def solution(mesh):
    in_specs = (
        P(None, "leaf"),
        P("leaf"),
        P("leaf", None, None),
        P("leaf", None, None),
        P("leaf", None),
        P("leaf", None, None, None),
        P("leaf", None),
        P("leaf"),
        P("leaf", None, None, None),
        P(),
        P(),
        P("leaf", None, None),
        P(),
    )
    out_specs = P(None, "leaf")
    return jax.shard_map(local, mesh=mesh, in_specs=in_specs, out_specs=out_specs, check_vma=False)
```

```python
import functools

import jax
import jax.numpy as jnp
from jax import lax
from jax.experimental import pallas as pl
from jax.experimental.pallas import tpu as pltpu
from jax.sharding import PartitionSpec as P

REACH = 4
DEPTH = 4
NODE_REACH = (1 << DEPTH) - 1

HIGHEST_PRECISION = lax.Precision.HIGHEST
OFFSETS = (-3, -2, 2, 3)
MESH_ID = pl.DeviceIdType.MESH


def nt_dot(x, y):
    return lax.dot_general(x, y, (((1,), (1,)), ((), ())), precision=HIGHEST_PRECISION,
                           preferred_element_type=jnp.float32)


def nn_dot(x, y):
    return jnp.dot(x, y, precision=HIGHEST_PRECISION, preferred_element_type=jnp.float32)


def up_level(nodes, t_even, t_odd):
    half, vectors, rank = nodes.shape[0] // 2, nodes.shape[1], nodes.shape[2]
    paired = nodes.reshape(half, 2 * vectors, rank)
    even = paired[:, :vectors].reshape(half * vectors, rank)
    odd = paired[:, vectors:].reshape(half * vectors, rank)
    return (nn_dot(even, t_even) + nn_dot(odd, t_odd)).reshape(half, vectors, rank)


def tree_kernel(count, top_count,
                x_ref, near_ref, transfer_ref, couple_ref, top_couple_ref,
                lift_ref, bases_ref, far_ref,
                links_ref, weight_ref, near_ids_ref, far_ids_ref, far_count_ref,
                near_out,
                node_buf, coef_buf, ext_buf, top_buf, lvl1, lvl2, own3, far3,
                send_sem, recv_sem, top_send, top_recv, third_send, third_recv):
    me = lax.axis_index("leaf")
    stride = count // top_count
    leaf_dev, leaf_size = lift_ref.shape[0], x_ref.shape[1] // lift_ref.shape[0]
    node_t = None
    for leaf in range(leaf_dev):
        coef_t = nt_dot(x_ref[:, pl.ds(leaf * leaf_size, leaf_size)], bases_ref[leaf])
        coef_buf[REACH * leaf_dev + leaf] = coef_t
        term = nn_dot(coef_t, lift_ref[leaf])
        node_t = term if node_t is None else node_t + term
    node_buf[NODE_REACH] = node_t
    node_ref = node_buf.at[NODE_REACH]
    coef_ref = coef_buf.at[pl.ds(REACH * leaf_dev, leaf_dev)]
    barrier = pltpu.get_barrier_semaphore()
    targets = []
    for k in range(1, NODE_REACH + 1):
        targets += [(me + k) % count, (me + count - k) % count]
    block3 = 1 << (DEPTH - 1)
    for offset in OFFSETS:
        targets.append((me + count - offset * block3) % count)
    for k in range(2, top_count - 1):
        targets.append((me + k * stride) % count)
    for dest in targets:
        pl.semaphore_signal(barrier, inc=1, device_id=(dest,), device_id_type=MESH_ID)
    pl.semaphore_wait(barrier, len(targets))

    copies = []

    def push(src, dst, dest):
        index = len(copies)
        copy = pltpu.make_async_remote_copy(
            src_ref=src, dst_ref=dst, send_sem=send_sem.at[index],
            recv_sem=recv_sem.at[index], device_id=(dest,), device_id_type=MESH_ID)
        copy.start()
        copies.append(copy)
        return copy

    block = 1 << DEPTH
    near_nodes = []
    for k in range(1, block):
        near_nodes.append(push(node_ref, node_buf.at[NODE_REACH - k], (me + k) % count))
        near_nodes.append(push(node_ref, node_buf.at[NODE_REACH + k], (me + count - k) % count))
    rest = []
    for k in range(1, REACH + 1):
        rest.append(push(coef_ref, coef_buf.at[pl.ds((REACH - k) * leaf_dev, leaf_dev)],
                         (me + k) % count))
        rest.append(push(coef_ref, coef_buf.at[pl.ds((REACH + k) * leaf_dev, leaf_dev)],
                         (me + count - k) % count))
    leaves, leaf_size = ext_buf.shape[0] - 2, ext_buf.shape[2]
    rest.append(push(x_ref.at[:, pl.ds((leaves - 1) * leaf_size, leaf_size)], ext_buf.at[0],
                     (me + 1) % count))
    rest.append(push(x_ref.at[:, pl.ds(0, leaf_size)], ext_buf.at[leaves + 1],
                     (me + count - 1) % count))
    for copy in near_nodes:
        copy.wait()

    own = node_buf[pl.ds(NODE_REACH - me % block, block)]
    for level in range(DEPTH - 1):
        own = up_level(own, transfer_ref[level, 0], transfer_ref[level, 1])
    own3[...] = own
    top_buf[0] = up_level(own, transfer_ref[DEPTH - 1, 0], transfer_ref[DEPTH - 1, 1])[0]
    mine3 = own3.at[(me >> (DEPTH - 1)) & 1]
    third = []
    for column, offset in enumerate(OFFSETS):
        copy = pltpu.make_async_remote_copy(
            src_ref=mine3, dst_ref=far3.at[column], send_sem=third_send.at[column],
            recv_sem=third_recv.at[column], device_id=((me + count - offset * block3) % count,),
            device_id_type=MESH_ID)
        copy.start()
        third.append(copy)
    top_copies = []
    for k in range(1, top_count):
        copy = pltpu.make_async_remote_copy(
            src_ref=top_buf.at[0], dst_ref=top_buf.at[k], send_sem=top_send.at[k - 1],
            recv_sem=top_recv.at[k - 1], device_id=((me + k * stride) % count,),
            device_id_type=MESH_ID)
        copy.start()
        top_copies.append(copy)

    for leaf in range(leaves):
        own_x = x_ref[:, pl.ds(leaf * leaf_size, leaf_size)]
        ext_buf[leaf + 1] = own_x
        near_out[:, pl.ds(leaf * leaf_size, leaf_size)] = nt_dot(own_x, near_ref[leaf, 0])

    for copy in rest:
        copy.wait()
    far_parts = []
    for leaf in range(leaf_dev):
        total = None
        for column in range(far_ref.shape[1]):
            far_id = far_ids_ref[leaf, column]
            slot = (far_id // leaf_dev - me + REACH) * leaf_dev + far_id % leaf_dev
            slot = jnp.minimum(jnp.maximum(slot, 0), (2 * REACH + 1) * leaf_dev - 1)
            scale = jnp.where(column < far_count_ref[leaf], 1.0, 0.0).astype(jnp.float32)
            partner = coef_buf[slot] * scale
            term = nt_dot(partner, far_ref[leaf, column])
            total = term if total is None else total + term
        far_parts.append(total)
    for leaf in range(leaves):
        total = near_out[:, pl.ds(leaf * leaf_size, leaf_size)]
        for column in range(1, near_ref.shape[1]):
            slot = near_ids_ref[column, leaf] - me * leaves + 1
            slot = jnp.minimum(jnp.maximum(slot, 0), leaves + 1)
            total = total + nt_dot(ext_buf[slot], near_ref[leaf, column])
        near_out[:, pl.ds(leaf * leaf_size, leaf_size)] = total

    span = 1 << (DEPTH - 2)
    low = me % span
    width = 7 * span
    start = NODE_REACH - 3 * span - low
    aligned = node_buf[pl.ds(start, width)]
    source = me - NODE_REACH + start + lax.broadcasted_iota(jnp.int32, aligned.shape, 0)
    aligned = jnp.where((source >= 0) & (source < count), aligned, 0.0)
    lvl1[...] = up_level(aligned, transfer_ref[0, 0], transfer_ref[0, 1])
    lvl2[...] = up_level(lvl1[...], transfer_ref[1, 0], transfer_ref[1, 1])
    for copy in third:
        copy.wait()

    couplings = []
    for level in range(DEPTH):
        centre = (low >> level) + ((3 * span) >> level)
        total = None
        for column, offset in enumerate(OFFSETS):
            if level == 0:
                partner = node_buf[NODE_REACH + offset]
                inside = (me + offset >= 0) & (me + offset < count)
                partner = jnp.where(inside, partner, 0.0)
            elif level == DEPTH - 1:
                partner = far3[column]
                inside = (me + offset * block3 >= 0) & (me + offset * block3 < count)
                partner = jnp.where(inside, partner, 0.0)
            else:
                partner = (lvl1, lvl2)[level - 1][centre + offset]
            scale = links_ref[level, column].astype(jnp.float32)
            term = nt_dot(partner, couple_ref[level, column]) * scale
            total = term if total is None else total + term
        couplings.append(total)

    for copy in top_copies:
        copy.wait()
    blended = top_buf[0] * weight_ref[0]
    for k in range(1, top_count):
        blended = blended + top_buf[k] * weight_ref[k]
    downward = nt_dot(blended, top_couple_ref[...])
    for level in reversed(range(DEPTH)):
        bit = (me >> level) & 1
        downward = couplings[level] + nt_dot(downward, transfer_ref[level, bit])
    for leaf in range(leaf_dev):
        leaf_out = nt_dot(downward, lift_ref[leaf]) + far_parts[leaf]
        where = pl.ds(leaf * leaf_size, leaf_size)
        near_out[:, where] = near_out[:, where] + nn_dot(leaf_out, bases_ref[leaf])


def tree_exchange(tree_x, near_blocks, transfer, couple, top_couple, lift, bases,
                  far_blocks, links, weights, near_ids, far_ids, far_count, count):
    top_count = count >> DEPTH
    n_copies = 2 + 2 * REACH + 2 * NODE_REACH
    span = 1 << (DEPTH - 2)
    vectors, rank = tree_x.shape[0], lift.shape[1]
    leaves, leaf_size = near_blocks.shape[0], near_blocks.shape[2]
    node_shape = (vectors, rank)
    vmem = pl.BlockSpec(memory_space=pltpu.VMEM)
    smem = pl.BlockSpec(memory_space=pltpu.SMEM)
    return pl.pallas_call(
        functools.partial(tree_kernel, count, top_count),
        out_shape=jax.ShapeDtypeStruct(tree_x.shape, jnp.float32),
        in_specs=[vmem] * 8 + [smem] * 5,
        out_specs=vmem,
        scratch_shapes=[
            pltpu.VMEM((2 * NODE_REACH + 1,) + node_shape, jnp.float32),
            pltpu.VMEM(((2 * REACH + 1) * leaves,) + node_shape, jnp.float32),
            pltpu.VMEM((leaves + 2, vectors, leaf_size), jnp.float32),
            pltpu.VMEM((top_count,) + node_shape, jnp.float32),
            pltpu.VMEM((7 * span // 2, vectors, rank), jnp.float32),
            pltpu.VMEM((7 * span // 4, vectors, rank), jnp.float32),
            pltpu.VMEM((2, vectors, rank), jnp.float32),
            pltpu.VMEM((len(OFFSETS), vectors, rank), jnp.float32),
            pltpu.SemaphoreType.DMA((n_copies,)),
            pltpu.SemaphoreType.DMA((n_copies,)),
            pltpu.SemaphoreType.DMA((top_count - 1,)),
            pltpu.SemaphoreType.DMA((top_count - 1,)),
            pltpu.SemaphoreType.DMA((len(OFFSETS),)),
            pltpu.SemaphoreType.DMA((len(OFFSETS),)),
        ],
        compiler_params=pltpu.CompilerParams(collective_id=0, has_side_effects=True),
    )(tree_x, near_blocks, transfer, couple, top_couple, lift, bases, far_blocks,
      links, weights, near_ids, far_ids, far_count)


def mat(m, x):
    return jnp.einsum("qr,rs->qs", m, x, precision=HIGHEST_PRECISION)


def up_pairs(transfer_level, nodes):
    paired = nodes.reshape(nodes.shape[0] // 2, 2, nodes.shape[1], nodes.shape[2])
    parent = jnp.einsum("rq,nrs->nqs", transfer_level[0], paired[:, 0], precision=HIGHEST_PRECISION)
    return parent + jnp.einsum("rq,nrs->nqs", transfer_level[1], paired[:, 1], precision=HIGHEST_PRECISION)


def local(
    points,
    order,
    bases,
    lift,
    near_ids,
    near_blocks,
    far_ids,
    far_count,
    far_blocks,
    transfer,
    couple,
    links,
    top_couple,
):
    position = lax.axis_index("leaf")
    count = lax.axis_size("leaf")
    vectors, points_dev = points.shape
    leaf_dev, leaf_size, rank_size = bases.shape
    local_order = order - position * points_dev
    tree_x = jnp.take(points, local_order, axis=1, mode="clip")
    blocks = tree_x.reshape(vectors, leaf_dev, leaf_size)
    top_count = count >> DEPTH
    top_index = position >> DEPTH
    ks = jnp.arange(top_count, dtype=jnp.int32)
    partner_index = (top_index - ks + top_count) % top_count
    distance = jnp.abs(partner_index - top_index)
    weights = jnp.where(distance >= 2, 1.0 / jnp.maximum(distance, 1).astype(jnp.float32), 0.0)
    tree_y = tree_exchange(
        tree_x, near_blocks, transfer, couple, top_couple, lift,
        jnp.swapaxes(bases, 1, 2), far_blocks, links[0], weights, near_ids.T, far_ids, far_count,
        count,
    )
    return jnp.zeros((vectors, points_dev), jnp.float32).at[:, local_order].set(tree_y, mode="clip")


def solution(mesh):
    in_specs = (
        P(None, "leaf"),
        P("leaf"),
        P("leaf", None, None),
        P("leaf", None, None),
        P("leaf", None),
        P("leaf", None, None, None),
        P("leaf", None),
        P("leaf"),
        P("leaf", None, None, None),
        P(),
        P(),
        P("leaf", None, None),
        P(),
    )
    out_specs = P(None, "leaf")
    return jax.shard_map(local, mesh=mesh, in_specs=in_specs, out_specs=out_specs, check_vma=False)
```

```python
import functools

import jax
import jax.numpy as jnp
from jax import lax
from jax.experimental import pallas as pl
from jax.experimental.pallas import tpu as pltpu
from jax.sharding import PartitionSpec as P

REACH = 4
DEPTH = 4
NODE_REACH = (1 << DEPTH) - 1

HIGHEST_PRECISION = lax.Precision.HIGHEST
KERNEL_PRECISION = lax.Precision.HIGH
OFFSETS = (-3, -2, 2, 3)
MESH_ID = pl.DeviceIdType.MESH


def nt_dot(x, y):
    return lax.dot_general(x, y, (((1,), (1,)), ((), ())), precision=KERNEL_PRECISION,
                           preferred_element_type=jnp.float32)


def nn_dot(x, y):
    return jnp.dot(x, y, precision=KERNEL_PRECISION, preferred_element_type=jnp.float32)


def up_level(nodes, t_even, t_odd):
    half, vectors, rank = nodes.shape[0] // 2, nodes.shape[1], nodes.shape[2]
    paired = nodes.reshape(half, 2 * vectors, rank)
    even = paired[:, :vectors].reshape(half * vectors, rank)
    odd = paired[:, vectors:].reshape(half * vectors, rank)
    return (nn_dot(even, t_even) + nn_dot(odd, t_odd)).reshape(half, vectors, rank)


def tree_kernel(count, top_count,
                x_ref, near_ref, transfer_ref, couple_ref, top_couple_ref,
                lift_ref, bases_ref, far_ref,
                links_ref, weight_ref, near_ids_ref, far_ids_ref, far_count_ref,
                near_out,
                node_buf, coef_buf, ext_buf, top_buf, lvl1, lvl2, own3, far3,
                send_sem, recv_sem, top_send, top_recv, third_send, third_recv):
    me = lax.axis_index("leaf")
    stride = count // top_count
    leaf_dev, leaf_size = lift_ref.shape[0], x_ref.shape[1] // lift_ref.shape[0]
    node_t = None
    for leaf in range(leaf_dev):
        coef_t = nt_dot(x_ref[:, pl.ds(leaf * leaf_size, leaf_size)], bases_ref[leaf])
        coef_buf[REACH * leaf_dev + leaf] = coef_t
        term = nn_dot(coef_t, lift_ref[leaf])
        node_t = term if node_t is None else node_t + term
    node_buf[NODE_REACH] = node_t
    node_ref = node_buf.at[NODE_REACH]
    coef_ref = coef_buf.at[pl.ds(REACH * leaf_dev, leaf_dev)]
    barrier = pltpu.get_barrier_semaphore()
    targets = []
    for k in range(1, NODE_REACH + 1):
        targets += [(me + k) % count, (me + count - k) % count]
    block3 = 1 << (DEPTH - 1)
    for offset in OFFSETS:
        targets.append((me + count - offset * block3) % count)
    for k in range(2, top_count - 1):
        targets.append((me + k * stride) % count)
    for dest in targets:
        pl.semaphore_signal(barrier, inc=1, device_id=(dest,), device_id_type=MESH_ID)
    pl.semaphore_wait(barrier, len(targets))

    copies = []

    def push(src, dst, dest):
        index = len(copies)
        copy = pltpu.make_async_remote_copy(
            src_ref=src, dst_ref=dst, send_sem=send_sem.at[index],
            recv_sem=recv_sem.at[index], device_id=(dest,), device_id_type=MESH_ID)
        copy.start()
        copies.append(copy)
        return copy

    block = 1 << DEPTH
    near_nodes = []
    for k in range(1, block):
        near_nodes.append(push(node_ref, node_buf.at[NODE_REACH - k], (me + k) % count))
        near_nodes.append(push(node_ref, node_buf.at[NODE_REACH + k], (me + count - k) % count))
    rest = []
    for k in range(1, REACH + 1):
        rest.append(push(coef_ref, coef_buf.at[pl.ds((REACH - k) * leaf_dev, leaf_dev)],
                         (me + k) % count))
        rest.append(push(coef_ref, coef_buf.at[pl.ds((REACH + k) * leaf_dev, leaf_dev)],
                         (me + count - k) % count))
    leaves, leaf_size = ext_buf.shape[0] - 2, ext_buf.shape[2]
    rest.append(push(x_ref.at[:, pl.ds((leaves - 1) * leaf_size, leaf_size)], ext_buf.at[0],
                     (me + 1) % count))
    rest.append(push(x_ref.at[:, pl.ds(0, leaf_size)], ext_buf.at[leaves + 1],
                     (me + count - 1) % count))
    for copy in near_nodes:
        copy.wait()

    own = node_buf[pl.ds(NODE_REACH - me % block, block)]
    for level in range(DEPTH - 1):
        own = up_level(own, transfer_ref[level, 0], transfer_ref[level, 1])
    own3[...] = own
    top_buf[0] = up_level(own, transfer_ref[DEPTH - 1, 0], transfer_ref[DEPTH - 1, 1])[0]
    mine3 = own3.at[(me >> (DEPTH - 1)) & 1]
    third = []
    for column, offset in enumerate(OFFSETS):
        copy = pltpu.make_async_remote_copy(
            src_ref=mine3, dst_ref=far3.at[column], send_sem=third_send.at[column],
            recv_sem=third_recv.at[column], device_id=((me + count - offset * block3) % count,),
            device_id_type=MESH_ID)
        copy.start()
        third.append(copy)
    top_copies = []
    for k in range(1, top_count):
        copy = pltpu.make_async_remote_copy(
            src_ref=top_buf.at[0], dst_ref=top_buf.at[k], send_sem=top_send.at[k - 1],
            recv_sem=top_recv.at[k - 1], device_id=((me + k * stride) % count,),
            device_id_type=MESH_ID)
        copy.start()
        top_copies.append(copy)

    for leaf in range(leaves):
        own_x = x_ref[:, pl.ds(leaf * leaf_size, leaf_size)]
        ext_buf[leaf + 1] = own_x
        near_out[:, pl.ds(leaf * leaf_size, leaf_size)] = nt_dot(own_x, near_ref[leaf, 0])

    for copy in rest:
        copy.wait()
    far_parts = []
    for leaf in range(leaf_dev):
        total = None
        for column in range(far_ref.shape[1]):
            far_id = far_ids_ref[leaf, column]
            slot = (far_id // leaf_dev - me + REACH) * leaf_dev + far_id % leaf_dev
            slot = jnp.minimum(jnp.maximum(slot, 0), (2 * REACH + 1) * leaf_dev - 1)
            scale = jnp.where(column < far_count_ref[leaf], 1.0, 0.0).astype(jnp.float32)
            partner = coef_buf[slot] * scale
            term = nt_dot(partner, far_ref[leaf, column])
            total = term if total is None else total + term
        far_parts.append(total)
    for leaf in range(leaves):
        total = near_out[:, pl.ds(leaf * leaf_size, leaf_size)]
        for column in range(1, near_ref.shape[1]):
            slot = near_ids_ref[column, leaf] - me * leaves + 1
            slot = jnp.minimum(jnp.maximum(slot, 0), leaves + 1)
            total = total + nt_dot(ext_buf[slot], near_ref[leaf, column])
        near_out[:, pl.ds(leaf * leaf_size, leaf_size)] = total

    span = 1 << (DEPTH - 2)
    low = me % span
    width = 7 * span
    start = NODE_REACH - 3 * span - low
    aligned = node_buf[pl.ds(start, width)]
    source = me - NODE_REACH + start + lax.broadcasted_iota(jnp.int32, aligned.shape, 0)
    aligned = jnp.where((source >= 0) & (source < count), aligned, 0.0)
    lvl1[...] = up_level(aligned, transfer_ref[0, 0], transfer_ref[0, 1])
    lvl2[...] = up_level(lvl1[...], transfer_ref[1, 0], transfer_ref[1, 1])
    for copy in third:
        copy.wait()

    couplings = []
    for level in range(DEPTH):
        centre = (low >> level) + ((3 * span) >> level)
        total = None
        for column, offset in enumerate(OFFSETS):
            if level == 0:
                partner = node_buf[NODE_REACH + offset]
                inside = (me + offset >= 0) & (me + offset < count)
                partner = jnp.where(inside, partner, 0.0)
            elif level == DEPTH - 1:
                partner = far3[column]
                inside = (me + offset * block3 >= 0) & (me + offset * block3 < count)
                partner = jnp.where(inside, partner, 0.0)
            else:
                partner = (lvl1, lvl2)[level - 1][centre + offset]
            scale = links_ref[level, column].astype(jnp.float32)
            term = nt_dot(partner, couple_ref[level, column]) * scale
            total = term if total is None else total + term
        couplings.append(total)

    for copy in top_copies:
        copy.wait()
    blended = top_buf[0] * weight_ref[0]
    for k in range(1, top_count):
        blended = blended + top_buf[k] * weight_ref[k]
    downward = nt_dot(blended, top_couple_ref[...])
    for level in reversed(range(DEPTH)):
        bit = (me >> level) & 1
        downward = couplings[level] + nt_dot(downward, transfer_ref[level, bit])
    for leaf in range(leaf_dev):
        leaf_out = nt_dot(downward, lift_ref[leaf]) + far_parts[leaf]
        where = pl.ds(leaf * leaf_size, leaf_size)
        near_out[:, where] = near_out[:, where] + nn_dot(leaf_out, bases_ref[leaf])


def tree_exchange(tree_x, near_blocks, transfer, couple, top_couple, lift, bases,
                  far_blocks, links, weights, near_ids, far_ids, far_count, count):
    top_count = count >> DEPTH
    n_copies = 2 + 2 * REACH + 2 * NODE_REACH
    span = 1 << (DEPTH - 2)
    vectors, rank = tree_x.shape[0], lift.shape[1]
    leaves, leaf_size = near_blocks.shape[0], near_blocks.shape[2]
    node_shape = (vectors, rank)
    vmem = pl.BlockSpec(memory_space=pltpu.VMEM)
    smem = pl.BlockSpec(memory_space=pltpu.SMEM)
    return pl.pallas_call(
        functools.partial(tree_kernel, count, top_count),
        out_shape=jax.ShapeDtypeStruct(tree_x.shape, jnp.float32),
        in_specs=[vmem] * 8 + [smem] * 5,
        out_specs=vmem,
        scratch_shapes=[
            pltpu.VMEM((2 * NODE_REACH + 1,) + node_shape, jnp.float32),
            pltpu.VMEM(((2 * REACH + 1) * leaves,) + node_shape, jnp.float32),
            pltpu.VMEM((leaves + 2, vectors, leaf_size), jnp.float32),
            pltpu.VMEM((top_count,) + node_shape, jnp.float32),
            pltpu.VMEM((7 * span // 2, vectors, rank), jnp.float32),
            pltpu.VMEM((7 * span // 4, vectors, rank), jnp.float32),
            pltpu.VMEM((2, vectors, rank), jnp.float32),
            pltpu.VMEM((len(OFFSETS), vectors, rank), jnp.float32),
            pltpu.SemaphoreType.DMA((n_copies,)),
            pltpu.SemaphoreType.DMA((n_copies,)),
            pltpu.SemaphoreType.DMA((top_count - 1,)),
            pltpu.SemaphoreType.DMA((top_count - 1,)),
            pltpu.SemaphoreType.DMA((len(OFFSETS),)),
            pltpu.SemaphoreType.DMA((len(OFFSETS),)),
        ],
        compiler_params=pltpu.CompilerParams(collective_id=0, has_side_effects=True),
    )(tree_x, near_blocks, transfer, couple, top_couple, lift, bases, far_blocks,
      links, weights, near_ids, far_ids, far_count)


def mat(m, x):
    return jnp.einsum("qr,rs->qs", m, x, precision=HIGHEST_PRECISION)


def up_pairs(transfer_level, nodes):
    paired = nodes.reshape(nodes.shape[0] // 2, 2, nodes.shape[1], nodes.shape[2])
    parent = jnp.einsum("rq,nrs->nqs", transfer_level[0], paired[:, 0], precision=HIGHEST_PRECISION)
    return parent + jnp.einsum("rq,nrs->nqs", transfer_level[1], paired[:, 1], precision=HIGHEST_PRECISION)


def local(
    points,
    order,
    bases,
    lift,
    near_ids,
    near_blocks,
    far_ids,
    far_count,
    far_blocks,
    transfer,
    couple,
    links,
    top_couple,
):
    position = lax.axis_index("leaf")
    count = lax.axis_size("leaf")
    vectors, points_dev = points.shape
    leaf_dev, leaf_size, rank_size = bases.shape
    local_order = order - position * points_dev
    tree_x = jnp.take(points, local_order, axis=1, mode="clip")
    blocks = tree_x.reshape(vectors, leaf_dev, leaf_size)
    top_count = count >> DEPTH
    top_index = position >> DEPTH
    ks = jnp.arange(top_count, dtype=jnp.int32)
    partner_index = (top_index - ks + top_count) % top_count
    distance = jnp.abs(partner_index - top_index)
    weights = jnp.where(distance >= 2, 1.0 / jnp.maximum(distance, 1).astype(jnp.float32), 0.0)
    tree_y = tree_exchange(
        tree_x, near_blocks, transfer, couple, top_couple, lift,
        jnp.swapaxes(bases, 1, 2), far_blocks, links[0], weights, near_ids.T, far_ids, far_count,
        count,
    )
    return jnp.zeros((vectors, points_dev), jnp.float32).at[:, local_order].set(tree_y, mode="clip")


def solution(mesh):
    in_specs = (
        P(None, "leaf"),
        P("leaf"),
        P("leaf", None, None),
        P("leaf", None, None),
        P("leaf", None),
        P("leaf", None, None, None),
        P("leaf", None),
        P("leaf"),
        P("leaf", None, None, None),
        P(),
        P(),
        P("leaf", None, None),
        P(),
    )
    out_specs = P(None, "leaf")
    return jax.shard_map(local, mesh=mesh, in_specs=in_specs, out_specs=out_specs, check_vma=False)
```

```python
import functools

import jax
import jax.numpy as jnp
from jax import lax
from jax.experimental import pallas as pl
from jax.experimental.pallas import tpu as pltpu
from jax.sharding import PartitionSpec as P

REACH = 4
DEPTH = 4
NODE_REACH = (1 << DEPTH) - 1

HIGHEST_PRECISION = lax.Precision.HIGHEST
KERNEL_PRECISION = lax.Precision.HIGH
OFFSETS = (-3, -2, 2, 3)
MESH_ID = pl.DeviceIdType.MESH


def nt_dot(x, y):
    return lax.dot_general(x, y, (((1,), (1,)), ((), ())), precision=KERNEL_PRECISION,
                           preferred_element_type=jnp.float32)


def nn_dot(x, y):
    return jnp.dot(x, y, precision=KERNEL_PRECISION, preferred_element_type=jnp.float32)


def up_level(nodes, t_even, t_odd):
    half, vectors, rank = nodes.shape[0] // 2, nodes.shape[1], nodes.shape[2]
    paired = nodes.reshape(half, 2 * vectors, rank)
    even = paired[:, :vectors].reshape(half * vectors, rank)
    odd = paired[:, vectors:].reshape(half * vectors, rank)
    return (nn_dot(even, t_even) + nn_dot(odd, t_odd)).reshape(half, vectors, rank)


def tree_kernel(count, top_count,
                x_ref, near_ref, transfer_ref, couple_ref, top_couple_ref,
                lift_ref, bases_ref, far_ref,
                links_ref, near_ids_ref, far_ids_ref, far_count_ref,
                near_out,
                node_buf, coef_buf, ext_buf, top_buf, lvl1, lvl2, own3, far3,
                send_sem, recv_sem, top_send, top_recv, third_send, third_recv):
    me = lax.axis_index("leaf")
    stride = count // top_count
    leaf_dev, leaf_size = lift_ref.shape[0], x_ref.shape[1] // lift_ref.shape[0]
    node_t = None
    for leaf in range(leaf_dev):
        coef_t = nt_dot(x_ref[:, pl.ds(leaf * leaf_size, leaf_size)], bases_ref[leaf])
        coef_buf[REACH * leaf_dev + leaf] = coef_t
        term = nn_dot(coef_t, lift_ref[leaf])
        node_t = term if node_t is None else node_t + term
    node_buf[NODE_REACH] = node_t
    node_ref = node_buf.at[NODE_REACH]
    coef_ref = coef_buf.at[pl.ds(REACH * leaf_dev, leaf_dev)]
    barrier = pltpu.get_barrier_semaphore()
    targets = []
    for k in range(1, NODE_REACH + 1):
        targets += [(me + k) % count, (me + count - k) % count]
    block3 = 1 << (DEPTH - 1)
    for offset in OFFSETS:
        targets.append((me + count - offset * block3) % count)
    for k in range(2, top_count - 1):
        targets.append((me + k * stride) % count)
    for dest in targets:
        pl.semaphore_signal(barrier, inc=1, device_id=(dest,), device_id_type=MESH_ID)
    pl.semaphore_wait(barrier, len(targets))

    copies = []

    def push(src, dst, dest):
        index = len(copies)
        copy = pltpu.make_async_remote_copy(
            src_ref=src, dst_ref=dst, send_sem=send_sem.at[index],
            recv_sem=recv_sem.at[index], device_id=(dest,), device_id_type=MESH_ID)
        copy.start()
        copies.append(copy)
        return copy

    block = 1 << DEPTH
    near_nodes = []
    for k in range(1, block):
        near_nodes.append(push(node_ref, node_buf.at[NODE_REACH - k], (me + k) % count))
        near_nodes.append(push(node_ref, node_buf.at[NODE_REACH + k], (me + count - k) % count))
    rest = []
    for k in range(1, REACH + 1):
        rest.append(push(coef_ref, coef_buf.at[pl.ds((REACH - k) * leaf_dev, leaf_dev)],
                         (me + k) % count))
        rest.append(push(coef_ref, coef_buf.at[pl.ds((REACH + k) * leaf_dev, leaf_dev)],
                         (me + count - k) % count))
    leaves, leaf_size = ext_buf.shape[0] - 2, ext_buf.shape[2]
    rest.append(push(x_ref.at[:, pl.ds((leaves - 1) * leaf_size, leaf_size)], ext_buf.at[0],
                     (me + 1) % count))
    rest.append(push(x_ref.at[:, pl.ds(0, leaf_size)], ext_buf.at[leaves + 1],
                     (me + count - 1) % count))
    for copy in near_nodes:
        copy.wait()

    own = node_buf[pl.ds(NODE_REACH - me % block, block)]
    for level in range(DEPTH - 1):
        own = up_level(own, transfer_ref[level, 0], transfer_ref[level, 1])
    own3[...] = own
    top_buf[0] = up_level(own, transfer_ref[DEPTH - 1, 0], transfer_ref[DEPTH - 1, 1])[0]
    mine3 = own3.at[(me >> (DEPTH - 1)) & 1]
    third = []
    for column, offset in enumerate(OFFSETS):
        copy = pltpu.make_async_remote_copy(
            src_ref=mine3, dst_ref=far3.at[column], send_sem=third_send.at[column],
            recv_sem=third_recv.at[column], device_id=((me + count - offset * block3) % count,),
            device_id_type=MESH_ID)
        copy.start()
        third.append(copy)
    top_copies = []
    for k in range(1, top_count):
        copy = pltpu.make_async_remote_copy(
            src_ref=top_buf.at[0], dst_ref=top_buf.at[k], send_sem=top_send.at[k - 1],
            recv_sem=top_recv.at[k - 1], device_id=((me + k * stride) % count,),
            device_id_type=MESH_ID)
        copy.start()
        top_copies.append(copy)

    for leaf in range(leaves):
        own_x = x_ref[:, pl.ds(leaf * leaf_size, leaf_size)]
        ext_buf[leaf + 1] = own_x
        near_out[:, pl.ds(leaf * leaf_size, leaf_size)] = nt_dot(own_x, near_ref[leaf, 0])

    for copy in rest:
        copy.wait()
    far_parts = []
    for leaf in range(leaf_dev):
        total = None
        for column in range(far_ref.shape[1]):
            far_id = far_ids_ref[leaf, column]
            slot = (far_id // leaf_dev - me + REACH) * leaf_dev + far_id % leaf_dev
            slot = jnp.minimum(jnp.maximum(slot, 0), (2 * REACH + 1) * leaf_dev - 1)
            scale = jnp.where(column < far_count_ref[leaf], 1.0, 0.0).astype(jnp.float32)
            partner = coef_buf[slot] * scale
            term = nt_dot(partner, far_ref[leaf, column])
            total = term if total is None else total + term
        far_parts.append(total)
    for leaf in range(leaves):
        total = near_out[:, pl.ds(leaf * leaf_size, leaf_size)]
        for column in range(1, near_ref.shape[1]):
            slot = near_ids_ref[column, leaf] - me * leaves + 1
            slot = jnp.minimum(jnp.maximum(slot, 0), leaves + 1)
            total = total + nt_dot(ext_buf[slot], near_ref[leaf, column])
        near_out[:, pl.ds(leaf * leaf_size, leaf_size)] = total

    span = 1 << (DEPTH - 2)
    low = me % span
    width = 7 * span
    start = NODE_REACH - 3 * span - low
    aligned = node_buf[pl.ds(start, width)]
    source = me - NODE_REACH + start + lax.broadcasted_iota(jnp.int32, aligned.shape, 0)
    aligned = jnp.where((source >= 0) & (source < count), aligned, 0.0)
    lvl1[...] = up_level(aligned, transfer_ref[0, 0], transfer_ref[0, 1])
    lvl2[...] = up_level(lvl1[...], transfer_ref[1, 0], transfer_ref[1, 1])
    for copy in third:
        copy.wait()

    couplings = []
    for level in range(DEPTH):
        centre = (low >> level) + ((3 * span) >> level)
        total = None
        for column, offset in enumerate(OFFSETS):
            if level == 0:
                partner = node_buf[NODE_REACH + offset]
                inside = (me + offset >= 0) & (me + offset < count)
                partner = jnp.where(inside, partner, 0.0)
            elif level == DEPTH - 1:
                partner = far3[column]
                inside = (me + offset * block3 >= 0) & (me + offset * block3 < count)
                partner = jnp.where(inside, partner, 0.0)
            else:
                partner = (lvl1, lvl2)[level - 1][centre + offset]
            scale = links_ref[level, column].astype(jnp.float32)
            term = nt_dot(partner, couple_ref[level, column]) * scale
            total = term if total is None else total + term
        couplings.append(total)

    for copy in top_copies:
        copy.wait()
    top_index = me // stride
    blended = None
    for k in range(top_count):
        other = (top_index - k + top_count) % top_count
        distance = jnp.maximum(top_index - other, other - top_index)
        spread = jnp.full(top_buf.shape[1:], jnp.maximum(distance, 1), jnp.int32)
        weight = jnp.where(distance >= 2, 1.0 / spread.astype(jnp.float32), 0.0)
        term = top_buf[k] * weight
        blended = term if blended is None else blended + term
    downward = nt_dot(blended, top_couple_ref[...])
    for level in reversed(range(DEPTH)):
        bit = (me >> level) & 1
        downward = couplings[level] + nt_dot(downward, transfer_ref[level, bit])
    for leaf in range(leaf_dev):
        leaf_out = nt_dot(downward, lift_ref[leaf]) + far_parts[leaf]
        where = pl.ds(leaf * leaf_size, leaf_size)
        near_out[:, where] = near_out[:, where] + nn_dot(leaf_out, bases_ref[leaf])


def tree_exchange(tree_x, near_blocks, transfer, couple, top_couple, lift, bases,
                  far_blocks, links, near_ids, far_ids, far_count, count):
    top_count = count >> DEPTH
    n_copies = 2 + 2 * REACH + 2 * NODE_REACH
    span = 1 << (DEPTH - 2)
    vectors, rank = tree_x.shape[0], lift.shape[1]
    leaves, leaf_size = near_blocks.shape[0], near_blocks.shape[2]
    node_shape = (vectors, rank)
    vmem = pl.BlockSpec(memory_space=pltpu.VMEM)
    smem = pl.BlockSpec(memory_space=pltpu.SMEM)
    return pl.pallas_call(
        functools.partial(tree_kernel, count, top_count),
        out_shape=jax.ShapeDtypeStruct(tree_x.shape, jnp.float32),
        in_specs=[vmem] * 8 + [smem] * 4,
        out_specs=vmem,
        scratch_shapes=[
            pltpu.VMEM((2 * NODE_REACH + 1,) + node_shape, jnp.float32),
            pltpu.VMEM(((2 * REACH + 1) * leaves,) + node_shape, jnp.float32),
            pltpu.VMEM((leaves + 2, vectors, leaf_size), jnp.float32),
            pltpu.VMEM((top_count,) + node_shape, jnp.float32),
            pltpu.VMEM((7 * span // 2, vectors, rank), jnp.float32),
            pltpu.VMEM((7 * span // 4, vectors, rank), jnp.float32),
            pltpu.VMEM((2, vectors, rank), jnp.float32),
            pltpu.VMEM((len(OFFSETS), vectors, rank), jnp.float32),
            pltpu.SemaphoreType.DMA((n_copies,)),
            pltpu.SemaphoreType.DMA((n_copies,)),
            pltpu.SemaphoreType.DMA((top_count - 1,)),
            pltpu.SemaphoreType.DMA((top_count - 1,)),
            pltpu.SemaphoreType.DMA((len(OFFSETS),)),
            pltpu.SemaphoreType.DMA((len(OFFSETS),)),
        ],
        compiler_params=pltpu.CompilerParams(collective_id=0, has_side_effects=True),
    )(tree_x, near_blocks, transfer, couple, top_couple, lift, bases, far_blocks,
      links, near_ids, far_ids, far_count)


def mat(m, x):
    return jnp.einsum("qr,rs->qs", m, x, precision=HIGHEST_PRECISION)


def up_pairs(transfer_level, nodes):
    paired = nodes.reshape(nodes.shape[0] // 2, 2, nodes.shape[1], nodes.shape[2])
    parent = jnp.einsum("rq,nrs->nqs", transfer_level[0], paired[:, 0], precision=HIGHEST_PRECISION)
    return parent + jnp.einsum("rq,nrs->nqs", transfer_level[1], paired[:, 1], precision=HIGHEST_PRECISION)


def local(
    points,
    order,
    bases,
    lift,
    near_ids,
    near_blocks,
    far_ids,
    far_count,
    far_blocks,
    transfer,
    couple,
    links,
    top_couple,
):
    position = lax.axis_index("leaf")
    count = lax.axis_size("leaf")
    vectors, points_dev = points.shape
    leaf_dev, leaf_size, rank_size = bases.shape
    local_order = order - position * points_dev
    tree_x = jnp.take(points, local_order, axis=1, mode="clip")
    blocks = tree_x.reshape(vectors, leaf_dev, leaf_size)
    tree_y = tree_exchange(
        tree_x, near_blocks, transfer, couple, top_couple, lift,
        jnp.swapaxes(bases, 1, 2), far_blocks, links[0], near_ids.T, far_ids, far_count,
        count,
    )
    return jnp.zeros((vectors, points_dev), jnp.float32).at[:, local_order].set(tree_y, mode="promise_in_bounds")


def solution(mesh):
    in_specs = (
        P(None, "leaf"),
        P("leaf"),
        P("leaf", None, None),
        P("leaf", None, None),
        P("leaf", None),
        P("leaf", None, None, None),
        P("leaf", None),
        P("leaf"),
        P("leaf", None, None, None),
        P(),
        P(),
        P("leaf", None, None),
        P(),
    )
    out_specs = P(None, "leaf")
    return jax.shard_map(local, mesh=mesh, in_specs=in_specs, out_specs=out_specs, check_vma=False)
```

```python
import functools

import jax
import jax.numpy as jnp
from jax import lax
from jax.experimental import pallas as pl
from jax.experimental.pallas import tpu as pltpu
from jax.sharding import PartitionSpec as P

REACH = 4
DEPTH = 4
NODE_REACH = (1 << DEPTH) - 1

HIGHEST_PRECISION = lax.Precision.HIGHEST
KERNEL_PRECISION = lax.Precision.HIGH
OFFSETS = (-3, -2, 2, 3)
MESH_ID = pl.DeviceIdType.MESH


def nt_dot(x, y):
    return lax.dot_general(x, y, (((1,), (1,)), ((), ())), precision=KERNEL_PRECISION,
                           preferred_element_type=jnp.float32)


def nn_dot(x, y):
    return jnp.dot(x, y, precision=KERNEL_PRECISION, preferred_element_type=jnp.float32)


def up_level(nodes, t_even, t_odd):
    half, vectors, rank = nodes.shape[0] // 2, nodes.shape[1], nodes.shape[2]
    paired = nodes.reshape(half, 2 * vectors, rank)
    even = paired[:, :vectors].reshape(half * vectors, rank)
    odd = paired[:, vectors:].reshape(half * vectors, rank)
    return (nn_dot(even, t_even) + nn_dot(odd, t_odd)).reshape(half, vectors, rank)


def tree_kernel(count, top_count,
                x_ref, near_ref, transfer_ref, couple_ref, top_couple_ref,
                lift_ref, bases_ref, far_ref,
                links_ref, near_ids_ref, far_ids_ref, far_count_ref,
                near_out,
                node_buf, coef_buf, ext_buf, top_buf, lvl1, lvl2, own3, far3,
                send_sem, recv_sem, top_send, top_recv, third_send, third_recv):
    me = lax.axis_index("leaf")
    stride = count // top_count
    leaf_dev, leaf_size = lift_ref.shape[0], x_ref.shape[1] // lift_ref.shape[0]
    node_t = None
    for leaf in range(leaf_dev):
        coef_t = nt_dot(x_ref[:, pl.ds(leaf * leaf_size, leaf_size)], bases_ref[leaf])
        coef_buf[REACH * leaf_dev + leaf] = coef_t
        term = nn_dot(coef_t, lift_ref[leaf])
        node_t = term if node_t is None else node_t + term
    node_buf[NODE_REACH] = node_t
    node_ref = node_buf.at[NODE_REACH]
    coef_ref = coef_buf.at[pl.ds(REACH * leaf_dev, leaf_dev)]
    barrier = pltpu.get_barrier_semaphore()
    targets = []
    for k in range(1, NODE_REACH + 1):
        targets += [(me + k) % count, (me + count - k) % count]
    block3 = 1 << (DEPTH - 1)
    for offset in OFFSETS:
        targets.append((me + count - offset * block3) % count)
    for k in range(2, top_count - 1):
        targets.append((me + k * stride) % count)
    for dest in targets:
        pl.semaphore_signal(barrier, inc=1, device_id=(dest,), device_id_type=MESH_ID)
    pl.semaphore_wait(barrier, len(targets))

    copies = []

    def push(src, dst, dest):
        index = len(copies)
        copy = pltpu.make_async_remote_copy(
            src_ref=src, dst_ref=dst, send_sem=send_sem.at[index],
            recv_sem=recv_sem.at[index], device_id=(dest,), device_id_type=MESH_ID)
        copy.start()
        copies.append(copy)
        return copy

    block = 1 << DEPTH
    near_nodes = []
    for k in range(1, block):
        near_nodes.append(push(node_ref, node_buf.at[NODE_REACH - k], (me + k) % count))
        near_nodes.append(push(node_ref, node_buf.at[NODE_REACH + k], (me + count - k) % count))
    rest = []
    for k in range(1, REACH + 1):
        rest.append(push(coef_ref, coef_buf.at[pl.ds((REACH - k) * leaf_dev, leaf_dev)],
                         (me + k) % count))
        rest.append(push(coef_ref, coef_buf.at[pl.ds((REACH + k) * leaf_dev, leaf_dev)],
                         (me + count - k) % count))
    leaves, leaf_size = ext_buf.shape[0] - 2, ext_buf.shape[2]
    rest.append(push(x_ref.at[:, pl.ds((leaves - 1) * leaf_size, leaf_size)], ext_buf.at[0],
                     (me + 1) % count))
    rest.append(push(x_ref.at[:, pl.ds(0, leaf_size)], ext_buf.at[leaves + 1],
                     (me + count - 1) % count))
    for copy in near_nodes:
        copy.wait()

    own = node_buf[pl.ds(NODE_REACH - me % block, block)]
    for level in range(DEPTH - 1):
        own = up_level(own, transfer_ref[level, 0], transfer_ref[level, 1])
    own3[...] = own
    top_buf[0] = up_level(own, transfer_ref[DEPTH - 1, 0], transfer_ref[DEPTH - 1, 1])[0]
    mine3 = own3.at[(me >> (DEPTH - 1)) & 1]
    third = []
    for column, offset in enumerate(OFFSETS):
        copy = pltpu.make_async_remote_copy(
            src_ref=mine3, dst_ref=far3.at[column], send_sem=third_send.at[column],
            recv_sem=third_recv.at[column], device_id=((me + count - offset * block3) % count,),
            device_id_type=MESH_ID)
        copy.start()
        third.append(copy)
    top_copies = []
    for k in range(1, top_count):
        copy = pltpu.make_async_remote_copy(
            src_ref=top_buf.at[0], dst_ref=top_buf.at[k], send_sem=top_send.at[k - 1],
            recv_sem=top_recv.at[k - 1], device_id=((me + k * stride) % count,),
            device_id_type=MESH_ID)
        copy.start()
        top_copies.append(copy)

    for leaf in range(leaves):
        own_x = x_ref[:, pl.ds(leaf * leaf_size, leaf_size)]
        ext_buf[leaf + 1] = own_x
        near_out[:, pl.ds(leaf * leaf_size, leaf_size)] = nt_dot(own_x, near_ref[leaf, 0])

    for copy in rest:
        copy.wait()
    far_parts = []
    for leaf in range(leaf_dev):
        total = None
        for column in range(far_ref.shape[1]):
            far_id = far_ids_ref[leaf, column]
            slot = (far_id // leaf_dev - me + REACH) * leaf_dev + far_id % leaf_dev
            slot = jnp.minimum(jnp.maximum(slot, 0), (2 * REACH + 1) * leaf_dev - 1)
            scale = jnp.where(column < far_count_ref[leaf], 1.0, 0.0).astype(jnp.float32)
            partner = coef_buf[slot] * scale
            term = nt_dot(partner, far_ref[leaf, column])
            total = term if total is None else total + term
        far_parts.append(total)
    for leaf in range(leaves):
        total = near_out[:, pl.ds(leaf * leaf_size, leaf_size)]
        for column in range(1, near_ref.shape[1]):
            slot = near_ids_ref[column, leaf] - me * leaves + 1
            slot = jnp.minimum(jnp.maximum(slot, 0), leaves + 1)
            total = total + nt_dot(ext_buf[slot], near_ref[leaf, column])
        near_out[:, pl.ds(leaf * leaf_size, leaf_size)] = total

    span = 1 << (DEPTH - 2)
    low = me % span
    width = 7 * span
    start = NODE_REACH - 3 * span - low
    aligned = node_buf[pl.ds(start, width)]
    source = me - NODE_REACH + start + lax.broadcasted_iota(jnp.int32, aligned.shape, 0)
    aligned = jnp.where((source >= 0) & (source < count), aligned, 0.0)
    lvl1[...] = up_level(aligned, transfer_ref[0, 0], transfer_ref[0, 1])
    lvl2[...] = up_level(lvl1[...], transfer_ref[1, 0], transfer_ref[1, 1])
    for copy in third:
        copy.wait()

    couplings = []
    for level in range(DEPTH):
        centre = (low >> level) + ((3 * span) >> level)
        total = None
        for column, offset in enumerate(OFFSETS):
            if level == 0:
                partner = node_buf[NODE_REACH + offset]
                inside = (me + offset >= 0) & (me + offset < count)
                partner = jnp.where(inside, partner, 0.0)
            elif level == DEPTH - 1:
                partner = far3[column]
                inside = (me + offset * block3 >= 0) & (me + offset * block3 < count)
                partner = jnp.where(inside, partner, 0.0)
            else:
                partner = (lvl1, lvl2)[level - 1][centre + offset]
            scale = links_ref[level, column].astype(jnp.float32)
            term = nt_dot(partner, couple_ref[level, column]) * scale
            total = term if total is None else total + term
        couplings.append(total)

    lifted = []
    for leaf in range(leaf_dev):
        where = pl.ds(leaf * leaf_size, leaf_size)
        near_out[:, where] = near_out[:, where] + nn_dot(far_parts[leaf], bases_ref[leaf])
        lifted.append(lax.dot_general(
            lift_ref[leaf], bases_ref[leaf], (((0,), (0,)), ((), ())),
            precision=KERNEL_PRECISION, preferred_element_type=jnp.float32))
    for copy in top_copies:
        copy.wait()
    top_index = me // stride
    blended = None
    for k in range(top_count):
        other = (top_index - k + top_count) % top_count
        distance = jnp.maximum(top_index - other, other - top_index)
        spread = jnp.full(top_buf.shape[1:], jnp.maximum(distance, 1), jnp.int32)
        weight = jnp.where(distance >= 2, 1.0 / spread.astype(jnp.float32), 0.0)
        term = top_buf[k] * weight
        blended = term if blended is None else blended + term
    downward = nt_dot(blended, top_couple_ref[...])
    for level in reversed(range(DEPTH)):
        bit = (me >> level) & 1
        downward = couplings[level] + nt_dot(downward, transfer_ref[level, bit])
    for leaf in range(leaf_dev):
        where = pl.ds(leaf * leaf_size, leaf_size)
        near_out[:, where] = near_out[:, where] + nn_dot(downward, lifted[leaf])


def tree_exchange(tree_x, near_blocks, transfer, couple, top_couple, lift, bases,
                  far_blocks, links, near_ids, far_ids, far_count, count):
    top_count = count >> DEPTH
    n_copies = 2 + 2 * REACH + 2 * NODE_REACH
    span = 1 << (DEPTH - 2)
    vectors, rank = tree_x.shape[0], lift.shape[1]
    leaves, leaf_size = near_blocks.shape[0], near_blocks.shape[2]
    node_shape = (vectors, rank)
    vmem = pl.BlockSpec(memory_space=pltpu.VMEM)
    smem = pl.BlockSpec(memory_space=pltpu.SMEM)
    return pl.pallas_call(
        functools.partial(tree_kernel, count, top_count),
        out_shape=jax.ShapeDtypeStruct(tree_x.shape, jnp.float32),
        in_specs=[vmem] * 8 + [smem] * 4,
        out_specs=vmem,
        scratch_shapes=[
            pltpu.VMEM((2 * NODE_REACH + 1,) + node_shape, jnp.float32),
            pltpu.VMEM(((2 * REACH + 1) * leaves,) + node_shape, jnp.float32),
            pltpu.VMEM((leaves + 2, vectors, leaf_size), jnp.float32),
            pltpu.VMEM((top_count,) + node_shape, jnp.float32),
            pltpu.VMEM((7 * span // 2, vectors, rank), jnp.float32),
            pltpu.VMEM((7 * span // 4, vectors, rank), jnp.float32),
            pltpu.VMEM((2, vectors, rank), jnp.float32),
            pltpu.VMEM((len(OFFSETS), vectors, rank), jnp.float32),
            pltpu.SemaphoreType.DMA((n_copies,)),
            pltpu.SemaphoreType.DMA((n_copies,)),
            pltpu.SemaphoreType.DMA((top_count - 1,)),
            pltpu.SemaphoreType.DMA((top_count - 1,)),
            pltpu.SemaphoreType.DMA((len(OFFSETS),)),
            pltpu.SemaphoreType.DMA((len(OFFSETS),)),
        ],
        compiler_params=pltpu.CompilerParams(collective_id=0, has_side_effects=True),
    )(tree_x, near_blocks, transfer, couple, top_couple, lift, bases, far_blocks,
      links, near_ids, far_ids, far_count)


def mat(m, x):
    return jnp.einsum("qr,rs->qs", m, x, precision=HIGHEST_PRECISION)


def up_pairs(transfer_level, nodes):
    paired = nodes.reshape(nodes.shape[0] // 2, 2, nodes.shape[1], nodes.shape[2])
    parent = jnp.einsum("rq,nrs->nqs", transfer_level[0], paired[:, 0], precision=HIGHEST_PRECISION)
    return parent + jnp.einsum("rq,nrs->nqs", transfer_level[1], paired[:, 1], precision=HIGHEST_PRECISION)


def local(
    points,
    order,
    bases,
    lift,
    near_ids,
    near_blocks,
    far_ids,
    far_count,
    far_blocks,
    transfer,
    couple,
    links,
    top_couple,
):
    position = lax.axis_index("leaf")
    count = lax.axis_size("leaf")
    vectors, points_dev = points.shape
    leaf_dev, leaf_size, rank_size = bases.shape
    local_order = order - position * points_dev
    tree_x = jnp.take(points, local_order, axis=1, mode="clip")
    blocks = tree_x.reshape(vectors, leaf_dev, leaf_size)
    tree_y = tree_exchange(
        tree_x, near_blocks, transfer, couple, top_couple, lift,
        jnp.swapaxes(bases, 1, 2), far_blocks, links[0], near_ids.T, far_ids, far_count,
        count,
    )
    return jnp.zeros((vectors, points_dev), jnp.float32).at[:, local_order].set(tree_y, mode="promise_in_bounds")


def solution(mesh):
    in_specs = (
        P(None, "leaf"),
        P("leaf"),
        P("leaf", None, None),
        P("leaf", None, None),
        P("leaf", None),
        P("leaf", None, None, None),
        P("leaf", None),
        P("leaf"),
        P("leaf", None, None, None),
        P(),
        P(),
        P("leaf", None, None),
        P(),
    )
    out_specs = P(None, "leaf")
    return jax.shard_map(local, mesh=mesh, in_specs=in_specs, out_specs=out_specs, check_vma=False)
```

```python
import functools

import jax
import jax.numpy as jnp
from jax import lax
from jax.experimental import pallas as pl
from jax.experimental.pallas import tpu as pltpu
from jax.sharding import PartitionSpec as P

REACH = 4
DEPTH = 4
NODE_REACH = (1 << DEPTH) - 1

HIGHEST_PRECISION = lax.Precision.HIGHEST
KERNEL_PRECISION = lax.Precision.HIGH
OFFSETS = (-3, -2, 2, 3)
MESH_ID = pl.DeviceIdType.MESH


def nt_dot(x, y):
    return lax.dot_general(x, y, (((1,), (1,)), ((), ())), precision=KERNEL_PRECISION,
                           preferred_element_type=jnp.float32)


def nn_dot(x, y):
    return jnp.dot(x, y, precision=KERNEL_PRECISION, preferred_element_type=jnp.float32)


def up_level(nodes, t_even, t_odd):
    half, vectors, rank = nodes.shape[0] // 2, nodes.shape[1], nodes.shape[2]
    paired = nodes.reshape(half, 2 * vectors, rank)
    even = paired[:, :vectors].reshape(half * vectors, rank)
    odd = paired[:, vectors:].reshape(half * vectors, rank)
    return (nn_dot(even, t_even) + nn_dot(odd, t_odd)).reshape(half, vectors, rank)


def tree_kernel(count, top_count,
                x_ref, near_ref, transfer_ref, couple_ref, top_couple_ref,
                lift_ref, bases_ref, far_ref,
                links_ref, near_ids_ref, far_ids_ref, far_count_ref,
                near_out,
                node_buf, coef_buf, ext_buf, top_buf, lvl1, lvl2, own3, far3,
                send_sem, recv_sem, top_send, top_recv, third_send, third_recv):
    me = lax.axis_index("leaf")
    stride = count // top_count
    leaf_dev, leaf_size = lift_ref.shape[0], x_ref.shape[1] // lift_ref.shape[0]
    node_t = None
    for leaf in range(leaf_dev):
        coef_t = nt_dot(x_ref[:, pl.ds(leaf * leaf_size, leaf_size)], bases_ref[leaf])
        coef_buf[REACH * leaf_dev + leaf] = coef_t
        term = nn_dot(coef_t, lift_ref[leaf])
        node_t = term if node_t is None else node_t + term
    node_buf[NODE_REACH] = node_t
    node_ref = node_buf.at[NODE_REACH]
    coef_ref = coef_buf.at[pl.ds(REACH * leaf_dev, leaf_dev)]
    barrier = pltpu.get_barrier_semaphore()
    targets = []
    for k in range(1, NODE_REACH + 1):
        targets += [(me + k) % count, (me + count - k) % count]
    block3 = 1 << (DEPTH - 1)
    for offset in OFFSETS:
        targets.append((me + count - offset * block3) % count)
    for k in range(2, top_count - 1):
        targets.append((me + k * stride) % count)
    for dest in targets:
        pl.semaphore_signal(barrier, inc=1, device_id=(dest,), device_id_type=MESH_ID)
    pl.semaphore_wait(barrier, len(targets))

    copies = []

    def push(src, dst, dest):
        index = len(copies)
        copy = pltpu.make_async_remote_copy(
            src_ref=src, dst_ref=dst, send_sem=send_sem.at[index],
            recv_sem=recv_sem.at[index], device_id=(dest,), device_id_type=MESH_ID)
        copy.start()
        copies.append(copy)
        return copy

    block = 1 << DEPTH
    near_nodes = []
    for k in range(1, block):
        near_nodes.append(push(node_ref, node_buf.at[NODE_REACH - k], (me + k) % count))
        near_nodes.append(push(node_ref, node_buf.at[NODE_REACH + k], (me + count - k) % count))
    rest = []
    for k in range(1, REACH + 1):
        rest.append(push(coef_ref, coef_buf.at[pl.ds((REACH - k) * leaf_dev, leaf_dev)],
                         (me + k) % count))
        rest.append(push(coef_ref, coef_buf.at[pl.ds((REACH + k) * leaf_dev, leaf_dev)],
                         (me + count - k) % count))
    leaves, leaf_size = ext_buf.shape[0] - 2, ext_buf.shape[2]
    rest.append(push(x_ref.at[:, pl.ds((leaves - 1) * leaf_size, leaf_size)], ext_buf.at[0],
                     (me + 1) % count))
    rest.append(push(x_ref.at[:, pl.ds(0, leaf_size)], ext_buf.at[leaves + 1],
                     (me + count - 1) % count))
    for copy in near_nodes:
        copy.wait()

    own = node_buf[pl.ds(NODE_REACH - me % block, block)]
    for level in range(DEPTH - 1):
        own = up_level(own, transfer_ref[level, 0], transfer_ref[level, 1])
    own3[...] = own
    top_buf[0] = up_level(own, transfer_ref[DEPTH - 1, 0], transfer_ref[DEPTH - 1, 1])[0]
    mine3 = own3.at[(me >> (DEPTH - 1)) & 1]
    third = []
    for column, offset in enumerate(OFFSETS):
        copy = pltpu.make_async_remote_copy(
            src_ref=mine3, dst_ref=far3.at[column], send_sem=third_send.at[column],
            recv_sem=third_recv.at[column], device_id=((me + count - offset * block3) % count,),
            device_id_type=MESH_ID)
        copy.start()
        third.append(copy)
    top_copies = []
    for k in range(1, top_count):
        copy = pltpu.make_async_remote_copy(
            src_ref=top_buf.at[0], dst_ref=top_buf.at[k], send_sem=top_send.at[k - 1],
            recv_sem=top_recv.at[k - 1], device_id=((me + k * stride) % count,),
            device_id_type=MESH_ID)
        copy.start()
        top_copies.append(copy)

    for leaf in range(leaves):
        own_x = x_ref[:, pl.ds(leaf * leaf_size, leaf_size)]
        ext_buf[leaf + 1] = own_x
        near_out[:, pl.ds(leaf * leaf_size, leaf_size)] = nt_dot(own_x, near_ref[leaf, 0])

    span = 1 << (DEPTH - 2)
    low = me % span
    width = 7 * span
    start = NODE_REACH - 3 * span - low
    aligned = node_buf[pl.ds(start, width)]
    source = me - NODE_REACH + start + lax.broadcasted_iota(jnp.int32, aligned.shape, 0)
    aligned = jnp.where((source >= 0) & (source < count), aligned, 0.0)
    lvl1[...] = up_level(aligned, transfer_ref[0, 0], transfer_ref[0, 1])
    lvl2[...] = up_level(lvl1[...], transfer_ref[1, 0], transfer_ref[1, 1])
    for copy in rest:
        copy.wait()
    far_parts = []
    for leaf in range(leaf_dev):
        total = None
        for column in range(far_ref.shape[1]):
            far_id = far_ids_ref[leaf, column]
            slot = (far_id // leaf_dev - me + REACH) * leaf_dev + far_id % leaf_dev
            slot = jnp.minimum(jnp.maximum(slot, 0), (2 * REACH + 1) * leaf_dev - 1)
            scale = jnp.where(column < far_count_ref[leaf], 1.0, 0.0).astype(jnp.float32)
            partner = coef_buf[slot] * scale
            term = nt_dot(partner, far_ref[leaf, column])
            total = term if total is None else total + term
        far_parts.append(total)
    for leaf in range(leaves):
        total = near_out[:, pl.ds(leaf * leaf_size, leaf_size)]
        for column in range(1, near_ref.shape[1]):
            slot = near_ids_ref[column, leaf] - me * leaves + 1
            slot = jnp.minimum(jnp.maximum(slot, 0), leaves + 1)
            total = total + nt_dot(ext_buf[slot], near_ref[leaf, column])
        near_out[:, pl.ds(leaf * leaf_size, leaf_size)] = total

    for copy in third:
        copy.wait()

    couplings = []
    for level in range(DEPTH):
        centre = (low >> level) + ((3 * span) >> level)
        total = None
        for column, offset in enumerate(OFFSETS):
            if level == 0:
                partner = node_buf[NODE_REACH + offset]
                inside = (me + offset >= 0) & (me + offset < count)
                partner = jnp.where(inside, partner, 0.0)
            elif level == DEPTH - 1:
                partner = far3[column]
                inside = (me + offset * block3 >= 0) & (me + offset * block3 < count)
                partner = jnp.where(inside, partner, 0.0)
            else:
                partner = (lvl1, lvl2)[level - 1][centre + offset]
            scale = links_ref[level, column].astype(jnp.float32)
            term = nt_dot(partner, couple_ref[level, column]) * scale
            total = term if total is None else total + term
        couplings.append(total)

    lifted = []
    for leaf in range(leaf_dev):
        where = pl.ds(leaf * leaf_size, leaf_size)
        near_out[:, where] = near_out[:, where] + nn_dot(far_parts[leaf], bases_ref[leaf])
        lifted.append(lax.dot_general(
            lift_ref[leaf], bases_ref[leaf], (((0,), (0,)), ((), ())),
            precision=KERNEL_PRECISION, preferred_element_type=jnp.float32))
    for copy in top_copies:
        copy.wait()
    top_index = me // stride
    blended = None
    for k in range(top_count):
        other = (top_index - k + top_count) % top_count
        distance = jnp.maximum(top_index - other, other - top_index)
        spread = jnp.full(top_buf.shape[1:], jnp.maximum(distance, 1), jnp.int32)
        weight = jnp.where(distance >= 2, 1.0 / spread.astype(jnp.float32), 0.0)
        term = top_buf[k] * weight
        blended = term if blended is None else blended + term
    downward = nt_dot(blended, top_couple_ref[...])
    for level in reversed(range(DEPTH)):
        bit = (me >> level) & 1
        downward = couplings[level] + nt_dot(downward, transfer_ref[level, bit])
    for leaf in range(leaf_dev):
        where = pl.ds(leaf * leaf_size, leaf_size)
        near_out[:, where] = near_out[:, where] + nn_dot(downward, lifted[leaf])


def tree_exchange(tree_x, near_blocks, transfer, couple, top_couple, lift, bases,
                  far_blocks, links, near_ids, far_ids, far_count, count):
    top_count = count >> DEPTH
    n_copies = 2 + 2 * REACH + 2 * NODE_REACH
    span = 1 << (DEPTH - 2)
    vectors, rank = tree_x.shape[0], lift.shape[1]
    leaves, leaf_size = near_blocks.shape[0], near_blocks.shape[2]
    node_shape = (vectors, rank)
    vmem = pl.BlockSpec(memory_space=pltpu.VMEM)
    smem = pl.BlockSpec(memory_space=pltpu.SMEM)
    return pl.pallas_call(
        functools.partial(tree_kernel, count, top_count),
        out_shape=jax.ShapeDtypeStruct(tree_x.shape, jnp.float32),
        in_specs=[vmem] * 8 + [smem] * 4,
        out_specs=vmem,
        scratch_shapes=[
            pltpu.VMEM((2 * NODE_REACH + 1,) + node_shape, jnp.float32),
            pltpu.VMEM(((2 * REACH + 1) * leaves,) + node_shape, jnp.float32),
            pltpu.VMEM((leaves + 2, vectors, leaf_size), jnp.float32),
            pltpu.VMEM((top_count,) + node_shape, jnp.float32),
            pltpu.VMEM((7 * span // 2, vectors, rank), jnp.float32),
            pltpu.VMEM((7 * span // 4, vectors, rank), jnp.float32),
            pltpu.VMEM((2, vectors, rank), jnp.float32),
            pltpu.VMEM((len(OFFSETS), vectors, rank), jnp.float32),
            pltpu.SemaphoreType.DMA((n_copies,)),
            pltpu.SemaphoreType.DMA((n_copies,)),
            pltpu.SemaphoreType.DMA((top_count - 1,)),
            pltpu.SemaphoreType.DMA((top_count - 1,)),
            pltpu.SemaphoreType.DMA((len(OFFSETS),)),
            pltpu.SemaphoreType.DMA((len(OFFSETS),)),
        ],
        compiler_params=pltpu.CompilerParams(collective_id=0, has_side_effects=True),
    )(tree_x, near_blocks, transfer, couple, top_couple, lift, bases, far_blocks,
      links, near_ids, far_ids, far_count)


def mat(m, x):
    return jnp.einsum("qr,rs->qs", m, x, precision=HIGHEST_PRECISION)


def up_pairs(transfer_level, nodes):
    paired = nodes.reshape(nodes.shape[0] // 2, 2, nodes.shape[1], nodes.shape[2])
    parent = jnp.einsum("rq,nrs->nqs", transfer_level[0], paired[:, 0], precision=HIGHEST_PRECISION)
    return parent + jnp.einsum("rq,nrs->nqs", transfer_level[1], paired[:, 1], precision=HIGHEST_PRECISION)


def local(
    points,
    order,
    bases,
    lift,
    near_ids,
    near_blocks,
    far_ids,
    far_count,
    far_blocks,
    transfer,
    couple,
    links,
    top_couple,
):
    position = lax.axis_index("leaf")
    count = lax.axis_size("leaf")
    vectors, points_dev = points.shape
    leaf_dev, leaf_size, rank_size = bases.shape
    local_order = order - position * points_dev
    tree_x = jnp.take(points, local_order, axis=1, mode="clip")
    blocks = tree_x.reshape(vectors, leaf_dev, leaf_size)
    tree_y = tree_exchange(
        tree_x, near_blocks, transfer, couple, top_couple, lift,
        jnp.swapaxes(bases, 1, 2), far_blocks, links[0], near_ids.T, far_ids, far_count,
        count,
    )
    return jnp.zeros((vectors, points_dev), jnp.float32).at[:, local_order].set(tree_y, mode="promise_in_bounds")


def solution(mesh):
    in_specs = (
        P(None, "leaf"),
        P("leaf"),
        P("leaf", None, None),
        P("leaf", None, None),
        P("leaf", None),
        P("leaf", None, None, None),
        P("leaf", None),
        P("leaf"),
        P("leaf", None, None, None),
        P(),
        P(),
        P("leaf", None, None),
        P(),
    )
    out_specs = P(None, "leaf")
    return jax.shard_map(local, mesh=mesh, in_specs=in_specs, out_specs=out_specs, check_vma=False)
```

```python
import functools

import jax
import jax.numpy as jnp
from jax import lax
from jax.experimental import pallas as pl
from jax.experimental.pallas import tpu as pltpu
from jax.sharding import PartitionSpec as P

REACH = 4
DEPTH = 4
NODE_REACH = (1 << DEPTH) - 1

HIGHEST_PRECISION = lax.Precision.HIGHEST
KERNEL_PRECISION = lax.Precision.HIGH
OFFSETS = (-3, -2, 2, 3)
MESH_ID = pl.DeviceIdType.MESH


def nt_dot(x, y):
    return lax.dot_general(x, y, (((1,), (1,)), ((), ())), precision=KERNEL_PRECISION,
                           preferred_element_type=jnp.float32)


def nn_dot(x, y):
    return jnp.dot(x, y, precision=KERNEL_PRECISION, preferred_element_type=jnp.float32)


def up_level(nodes, t_even, t_odd):
    half, vectors, rank = nodes.shape[0] // 2, nodes.shape[1], nodes.shape[2]
    paired = nodes.reshape(half, 2 * vectors, rank)
    even = paired[:, :vectors].reshape(half * vectors, rank)
    odd = paired[:, vectors:].reshape(half * vectors, rank)
    return (nn_dot(even, t_even) + nn_dot(odd, t_odd)).reshape(half, vectors, rank)


def tree_kernel(count, top_count,
                x_ref, near_ref, transfer_ref, couple_ref, top_couple_ref,
                lift_ref, bases_ref, far_ref,
                links_ref, near_ids_ref, far_ids_ref, far_count_ref,
                near_out,
                node_buf, coef_buf, ext_buf, top_buf, lvl1, lvl2, own3, far3,
                send_sem, recv_sem, top_send, top_recv, third_send, third_recv):
    me = lax.axis_index("leaf")
    stride = count // top_count
    leaf_dev, leaf_size = lift_ref.shape[0], x_ref.shape[1] // lift_ref.shape[0]
    node_t = None
    for leaf in range(leaf_dev):
        coef_t = nt_dot(x_ref[:, pl.ds(leaf * leaf_size, leaf_size)], bases_ref[leaf])
        coef_buf[REACH * leaf_dev + leaf] = coef_t
        term = nn_dot(coef_t, lift_ref[leaf])
        node_t = term if node_t is None else node_t + term
    node_buf[NODE_REACH] = node_t
    node_ref = node_buf.at[NODE_REACH]
    coef_ref = coef_buf.at[pl.ds(REACH * leaf_dev, leaf_dev)]
    barrier = pltpu.get_barrier_semaphore()
    targets = []
    for k in range(1, NODE_REACH + 1):
        targets += [(me + k) % count, (me + count - k) % count]
    block3 = 1 << (DEPTH - 1)
    for offset in OFFSETS:
        targets.append((me + count - offset * block3) % count)
    for k in range(2, top_count - 1):
        targets.append((me + k * stride) % count)
    for dest in targets:
        pl.semaphore_signal(barrier, inc=1, device_id=(dest,), device_id_type=MESH_ID)
    pl.semaphore_wait(barrier, len(targets))

    copies = []

    def push(src, dst, dest):
        index = len(copies)
        copy = pltpu.make_async_remote_copy(
            src_ref=src, dst_ref=dst, send_sem=send_sem.at[index],
            recv_sem=recv_sem.at[index], device_id=(dest,), device_id_type=MESH_ID)
        copy.start()
        copies.append(copy)
        return copy

    block = 1 << DEPTH
    near_nodes = []
    for k in range(1, block):
        near_nodes.append(push(node_ref, node_buf.at[NODE_REACH - k], (me + k) % count))
        near_nodes.append(push(node_ref, node_buf.at[NODE_REACH + k], (me + count - k) % count))
    rest = []
    for k in range(1, REACH + 1):
        rest.append(push(coef_ref, coef_buf.at[pl.ds((REACH - k) * leaf_dev, leaf_dev)],
                         (me + k) % count))
        rest.append(push(coef_ref, coef_buf.at[pl.ds((REACH + k) * leaf_dev, leaf_dev)],
                         (me + count - k) % count))
    leaves, leaf_size = ext_buf.shape[0] - 2, ext_buf.shape[2]
    rest.append(push(x_ref.at[:, pl.ds((leaves - 1) * leaf_size, leaf_size)], ext_buf.at[0],
                     (me + 1) % count))
    rest.append(push(x_ref.at[:, pl.ds(0, leaf_size)], ext_buf.at[leaves + 1],
                     (me + count - 1) % count))
    for copy in near_nodes:
        copy.wait()

    own = node_buf[pl.ds(NODE_REACH - me % block, block)]
    for level in range(DEPTH - 1):
        own = up_level(own, transfer_ref[level, 0], transfer_ref[level, 1])
    own3[...] = own
    top_buf[0] = up_level(own, transfer_ref[DEPTH - 1, 0], transfer_ref[DEPTH - 1, 1])[0]
    mine3 = own3.at[(me >> (DEPTH - 1)) & 1]
    third = []
    for column, offset in enumerate(OFFSETS):
        copy = pltpu.make_async_remote_copy(
            src_ref=mine3, dst_ref=far3.at[column], send_sem=third_send.at[column],
            recv_sem=third_recv.at[column], device_id=((me + count - offset * block3) % count,),
            device_id_type=MESH_ID)
        copy.start()
        third.append(copy)
    top_copies = []
    for k in range(1, top_count):
        copy = pltpu.make_async_remote_copy(
            src_ref=top_buf.at[0], dst_ref=top_buf.at[k], send_sem=top_send.at[k - 1],
            recv_sem=top_recv.at[k - 1], device_id=((me + k * stride) % count,),
            device_id_type=MESH_ID)
        copy.start()
        top_copies.append(copy)

    for leaf in range(leaves):
        own_x = x_ref[:, pl.ds(leaf * leaf_size, leaf_size)]
        ext_buf[leaf + 1] = own_x
        near_out[:, pl.ds(leaf * leaf_size, leaf_size)] = nt_dot(own_x, near_ref[leaf, 0])

    span = 1 << (DEPTH - 2)
    low = me % span
    width = 7 * span
    start = NODE_REACH - 3 * span - low
    aligned = node_buf[pl.ds(start, width)]
    source = me - NODE_REACH + start + lax.broadcasted_iota(jnp.int32, aligned.shape, 0)
    aligned = jnp.where((source >= 0) & (source < count), aligned, 0.0)
    lvl1[...] = up_level(aligned, transfer_ref[0, 0], transfer_ref[0, 1])
    lvl2[...] = up_level(lvl1[...], transfer_ref[1, 0], transfer_ref[1, 1])
    def coupling(level):
        centre = (low >> level) + ((3 * span) >> level)
        total = None
        for column, offset in enumerate(OFFSETS):
            if level == 0:
                partner = node_buf[NODE_REACH + offset]
                inside = (me + offset >= 0) & (me + offset < count)
                partner = jnp.where(inside, partner, 0.0)
            elif level == DEPTH - 1:
                partner = far3[column]
                inside = (me + offset * block3 >= 0) & (me + offset * block3 < count)
                partner = jnp.where(inside, partner, 0.0)
            else:
                partner = (lvl1, lvl2)[level - 1][centre + offset]
            scale = links_ref[level, column].astype(jnp.float32)
            term = nt_dot(partner, couple_ref[level, column]) * scale
            total = term if total is None else total + term
        return total
    couplings = [coupling(level) for level in range(DEPTH - 1)]
    for copy in rest:
        copy.wait()
    far_parts = []
    for leaf in range(leaf_dev):
        total = None
        for column in range(far_ref.shape[1]):
            far_id = far_ids_ref[leaf, column]
            slot = (far_id // leaf_dev - me + REACH) * leaf_dev + far_id % leaf_dev
            slot = jnp.minimum(jnp.maximum(slot, 0), (2 * REACH + 1) * leaf_dev - 1)
            scale = jnp.where(column < far_count_ref[leaf], 1.0, 0.0).astype(jnp.float32)
            partner = coef_buf[slot] * scale
            term = nt_dot(partner, far_ref[leaf, column])
            total = term if total is None else total + term
        far_parts.append(total)
    for leaf in range(leaves):
        total = near_out[:, pl.ds(leaf * leaf_size, leaf_size)]
        for column in range(1, near_ref.shape[1]):
            slot = near_ids_ref[column, leaf] - me * leaves + 1
            slot = jnp.minimum(jnp.maximum(slot, 0), leaves + 1)
            total = total + nt_dot(ext_buf[slot], near_ref[leaf, column])
        near_out[:, pl.ds(leaf * leaf_size, leaf_size)] = total

    for copy in third:
        copy.wait()

    couplings.append(coupling(DEPTH - 1))

    lifted = []
    for leaf in range(leaf_dev):
        where = pl.ds(leaf * leaf_size, leaf_size)
        near_out[:, where] = near_out[:, where] + nn_dot(far_parts[leaf], bases_ref[leaf])
        lifted.append(lax.dot_general(
            lift_ref[leaf], bases_ref[leaf], (((0,), (0,)), ((), ())),
            precision=KERNEL_PRECISION, preferred_element_type=jnp.float32))
    for copy in top_copies:
        copy.wait()
    top_index = me // stride
    blended = None
    for k in range(top_count):
        other = (top_index - k + top_count) % top_count
        distance = jnp.maximum(top_index - other, other - top_index)
        spread = jnp.full(top_buf.shape[1:], jnp.maximum(distance, 1), jnp.int32)
        weight = jnp.where(distance >= 2, 1.0 / spread.astype(jnp.float32), 0.0)
        term = top_buf[k] * weight
        blended = term if blended is None else blended + term
    downward = nt_dot(blended, top_couple_ref[...])
    for level in reversed(range(DEPTH)):
        bit = (me >> level) & 1
        downward = couplings[level] + nt_dot(downward, transfer_ref[level, bit])
    for leaf in range(leaf_dev):
        where = pl.ds(leaf * leaf_size, leaf_size)
        near_out[:, where] = near_out[:, where] + nn_dot(downward, lifted[leaf])


def tree_exchange(tree_x, near_blocks, transfer, couple, top_couple, lift, bases,
                  far_blocks, links, near_ids, far_ids, far_count, count):
    top_count = count >> DEPTH
    n_copies = 2 + 2 * REACH + 2 * NODE_REACH
    span = 1 << (DEPTH - 2)
    vectors, rank = tree_x.shape[0], lift.shape[1]
    leaves, leaf_size = near_blocks.shape[0], near_blocks.shape[2]
    node_shape = (vectors, rank)
    vmem = pl.BlockSpec(memory_space=pltpu.VMEM)
    smem = pl.BlockSpec(memory_space=pltpu.SMEM)
    return pl.pallas_call(
        functools.partial(tree_kernel, count, top_count),
        out_shape=jax.ShapeDtypeStruct(tree_x.shape, jnp.float32),
        in_specs=[vmem] * 8 + [smem] * 4,
        out_specs=vmem,
        scratch_shapes=[
            pltpu.VMEM((2 * NODE_REACH + 1,) + node_shape, jnp.float32),
            pltpu.VMEM(((2 * REACH + 1) * leaves,) + node_shape, jnp.float32),
            pltpu.VMEM((leaves + 2, vectors, leaf_size), jnp.float32),
            pltpu.VMEM((top_count,) + node_shape, jnp.float32),
            pltpu.VMEM((7 * span // 2, vectors, rank), jnp.float32),
            pltpu.VMEM((7 * span // 4, vectors, rank), jnp.float32),
            pltpu.VMEM((2, vectors, rank), jnp.float32),
            pltpu.VMEM((len(OFFSETS), vectors, rank), jnp.float32),
            pltpu.SemaphoreType.DMA((n_copies,)),
            pltpu.SemaphoreType.DMA((n_copies,)),
            pltpu.SemaphoreType.DMA((top_count - 1,)),
            pltpu.SemaphoreType.DMA((top_count - 1,)),
            pltpu.SemaphoreType.DMA((len(OFFSETS),)),
            pltpu.SemaphoreType.DMA((len(OFFSETS),)),
        ],
        compiler_params=pltpu.CompilerParams(collective_id=0, has_side_effects=True),
    )(tree_x, near_blocks, transfer, couple, top_couple, lift, bases, far_blocks,
      links, near_ids, far_ids, far_count)


def mat(m, x):
    return jnp.einsum("qr,rs->qs", m, x, precision=HIGHEST_PRECISION)


def up_pairs(transfer_level, nodes):
    paired = nodes.reshape(nodes.shape[0] // 2, 2, nodes.shape[1], nodes.shape[2])
    parent = jnp.einsum("rq,nrs->nqs", transfer_level[0], paired[:, 0], precision=HIGHEST_PRECISION)
    return parent + jnp.einsum("rq,nrs->nqs", transfer_level[1], paired[:, 1], precision=HIGHEST_PRECISION)


def local(
    points,
    order,
    bases,
    lift,
    near_ids,
    near_blocks,
    far_ids,
    far_count,
    far_blocks,
    transfer,
    couple,
    links,
    top_couple,
):
    position = lax.axis_index("leaf")
    count = lax.axis_size("leaf")
    vectors, points_dev = points.shape
    leaf_dev, leaf_size, rank_size = bases.shape
    local_order = order - position * points_dev
    tree_x = jnp.take(points, local_order, axis=1, mode="clip")
    blocks = tree_x.reshape(vectors, leaf_dev, leaf_size)
    tree_y = tree_exchange(
        tree_x, near_blocks, transfer, couple, top_couple, lift,
        jnp.swapaxes(bases, 1, 2), far_blocks, links[0], near_ids.T, far_ids, far_count,
        count,
    )
    return jnp.zeros((vectors, points_dev), jnp.float32).at[:, local_order].set(tree_y, mode="promise_in_bounds")


def solution(mesh):
    in_specs = (
        P(None, "leaf"),
        P("leaf"),
        P("leaf", None, None),
        P("leaf", None, None),
        P("leaf", None),
        P("leaf", None, None, None),
        P("leaf", None),
        P("leaf"),
        P("leaf", None, None, None),
        P(),
        P(),
        P("leaf", None, None),
        P(),
    )
    out_specs = P(None, "leaf")
    return jax.shard_map(local, mesh=mesh, in_specs=in_specs, out_specs=out_specs, check_vma=False)
```
